32 devices in a mesh: grid: 1, samp: 32 (over z, y, x, core).
Axes of the slice: x: 2, y: 2, z: 4, core: 2. Of those that a mesh axis runs over, the one named last changes fastest.
Arguments:
- summary: bfloat16 [65536, 1024], P('samp'), may hold values from -10 to 10
- kernel: bfloat16 [1024, 4096], P(None, 'grid'), may hold values from -1 to 1
- grid_offset: float32 [4096], P('grid'), may hold values from -130 to 130
- log_prior: float32 [65536], P('samp'), may hold values from -6 to 6
- tile_event: int32 [512], P('samp'), may hold values from 0 to 63, as said below
- tile_live: int32 [512], P('samp'), may hold values from 2 to 128
Outputs:
- log_evidence: float32 [64, 4096], P('samp', 'grid')
- ess_fraction: float32 [64, 4096], P('samp', 'grid')
- log_posterior: float32 [4096], P('grid')
The draws below stay inside these ranges and needn't reach their ends.
Inputs may be any that keep to these rules, and one draw needn't show every extreme that they name: `tile_event`: every event owns at least one tile.
All inputs are finite; a program needn't handle non-finite values.
Results may differ from the reference program's by a relative error of at most 0.0003.
Values sent between devices are 32-bit elements; how exact they have to be, the bound alone decides.
No kernel may reach another device: no remote copies, remote signals or barrier semaphores. Data moves between devices by JAX's collectives and lax.ppermute only.
A program may use at most 128 MiB of HBM per device.

```python
import jax
import jax.numpy as jnp
from jax import lax

BINS = 1024
GRID = 4096
EVENTS = 64
TILE = 128
ROWS_DEV = 2048
TILES_DEV = 16
SAMPLES = 65536
TILES = 512
N_SAMP = 32


def kernel_table(key):
    raw = jax.random.normal(jax.random.fold_in(key, 101), (BINS, GRID), jnp.float32)
    return jnp.clip(raw, -4.0, 4.0) / jnp.sqrt(jnp.float32(BINS))


def draw_kernel(key, part):
    return kernel_table(key).astype(jnp.bfloat16)


def draw_summary(key, part):
    table = kernel_table(key)
    noise = jnp.clip(jax.random.normal(jax.random.fold_in(key, 202), (SAMPLES, BINS), jnp.float32), -6.0, 6.0)
    column = jax.random.randint(jax.random.fold_in(key, 303), (TILES,), 0, GRID, dtype=jnp.int32)
    strength = jnp.exp(jax.random.uniform(jax.random.fold_in(key, 404), (TILES,), jnp.float32, jnp.log(0.5), jnp.log(10.0)))
    chosen = jnp.take(table, column, axis=1).T
    pattern = jnp.where(chosen >= 0.0, jnp.float32(1.0), jnp.float32(-1.0))
    top_score = strength * jnp.sum(jnp.abs(chosen), axis=1)
    lower = 1.0 - 2.0 / top_score
    row_zero = strength[:, None] * pattern
    row_one = row_zero * lower[:, None]
    shaped = noise.reshape(TILES, TILE, BINS)
    shaped = shaped.at[:, 0, :].set(row_zero)
    shaped = shaped.at[:, 1, :].set(row_one)
    return shaped.reshape(SAMPLES, BINS).astype(jnp.bfloat16)


def draw_grid_offset(key, part):
    return jnp.clip(jax.random.normal(key, (GRID,), jnp.float32), -6.0, 6.0)


def draw_tile_event(key, part):
    first_key = jax.random.fold_in(key, 11)
    second_key = jax.random.fold_in(key, 23)
    extra = jax.random.randint(first_key, (TILES - EVENTS,), 0, EVENTS, dtype=jnp.int32)
    listing = jnp.concatenate([jnp.arange(EVENTS, dtype=jnp.int32), extra])
    return jax.random.permutation(second_key, listing).astype(jnp.int32)


def touch_ends(array, own_key, low, high):
    spot = [jax.random.randint(jax.random.fold_in(own_key, axis), (), 0, length) for axis, length in enumerate(array.shape)]
    widest = array.shape.index(max(array.shape))
    beside = spot[:widest] + [(spot[widest] + 1) % array.shape[widest]] + spot[widest + 1:]
    return array.at[tuple(spot)].set(low).at[tuple(beside)].set(high)


def level_of(key, extent, split, smallest, high):
    level, own = 1.0, jax.random.fold_in(key, 6)
    for dim, parts in split:
        heights = jnp.exp(jax.random.uniform(jax.random.fold_in(own, dim), (parts,), jnp.float32, smallest / len(split), high / len(split)))
        level = level * jnp.repeat(heights, extent[dim] // parts).reshape([-1 if axis == dim else 1 for axis in range(len(extent))])
    return level


def scatter_about(key, shape, scale, reach, split=(), kind=jnp.bfloat16):
    loudness = level_of(key, shape, split, -0.22, 0.18) if split else 1.0
    entries = jax.random.normal(key, shape, jnp.float32) * scale * loudness
    return jnp.minimum(jnp.maximum(entries, -reach), reach).astype(kind)


def setup_inputs(seed: int = 0) -> dict:
    splits = jax.random.split(jax.random.key(seed), 7)
    summary = draw_summary(jax.random.fold_in(splits[6], 71), 0)
    kernel = draw_kernel(jax.random.fold_in(splits[6], 71), 0)
    grid_offset = draw_grid_offset(jax.random.fold_in(splits[6], 71), 0)
    log_prior = scatter_about(splits[3], (SAMPLES,), 1.0, 6.0, ((0, 32),), jnp.float32)
    tile_event = draw_tile_event(jax.random.fold_in(splits[6], 71), 0)
    tile_live = touch_ends(jax.random.randint(splits[5], (TILES,), 2, TILE + 1), jax.random.fold_in(splits[5], 1), 2, TILE).astype(jnp.int32)
    return {"summary": summary, "kernel": kernel, "grid_offset": grid_offset, "log_prior": log_prior, "tile_event": tile_event, "tile_live": tile_live}


def reference(summary, kernel, grid_offset, log_prior, tile_event, tile_live):
    def block_stats(packed):
        block_rows, block_prior, block_live = packed
        scores = jnp.dot(block_rows, kernel, preferred_element_type=jnp.float32)
        scores = scores + grid_offset[None, :] - block_prior[:, None]
        scores = scores.reshape(TILES_DEV, TILE, GRID)
        is_live = lax.broadcasted_iota(jnp.int32, (TILES_DEV, TILE), 1) < block_live[:, None]
        masked = jnp.where(is_live[:, :, None], scores, jnp.float32(-1e30))
        tile_max = jnp.max(masked, axis=1)
        shifted = jnp.exp(masked - tile_max[:, None, :])
        return tile_max, jnp.sum(shifted, axis=1), jnp.sum(shifted * shifted, axis=1)

    tile_max, tile_first, tile_second = lax.map(block_stats, (summary.reshape(N_SAMP, ROWS_DEV, BINS), log_prior.reshape(N_SAMP, ROWS_DEV), tile_live.reshape(N_SAMP, TILES_DEV)))
    tile_max = tile_max.reshape(TILES, GRID)
    tile_first = tile_first.reshape(TILES, GRID)
    tile_second = tile_second.reshape(TILES, GRID)

    def event_stats(event_id):
        member = tile_event == event_id
        event_max = jnp.max(jnp.where(member[:, None], tile_max, jnp.float32(-1e30)), axis=0)
        factor = jnp.exp(tile_max - event_max[None, :])
        first_sum = jnp.sum(jnp.where(member[:, None], tile_first * factor, jnp.float32(0.0)), axis=0)
        second_sum = jnp.sum(jnp.where(member[:, None], tile_second * factor * factor, jnp.float32(0.0)), axis=0)
        live_count = jnp.sum(jnp.where(member, tile_live, 0)).astype(jnp.float32)
        evidence = event_max + jnp.log(first_sum) - jnp.log(live_count)
        return evidence, first_sum * first_sum / (second_sum * live_count)

    log_evidence, ess_fraction = lax.map(event_stats, jnp.arange(EVENTS, dtype=jnp.int32))
    loglik = jnp.sum(log_evidence, axis=0) / jnp.float32(EVENTS)
    grid_top = jnp.max(loglik)
    log_norm = grid_top + jnp.log(jnp.sum(jnp.exp(loglik - grid_top)))
    return log_evidence, ess_fraction, loglik - log_norm
```

```python
import functools

import jax
import jax.numpy as jnp
from jax import lax
from jax.experimental import pallas as pl
from jax.experimental.pallas import tpu as pltpu
from jax.sharding import PartitionSpec as P

EVENTS = 64
LANES = 128
GROUP = 16
CHUNK = 256
BLOCK = 512
NEG = -1e30
DEAD = 1e30


def stats_kernel(
    tiles, tile_rows, depth, cols, event_ref, live_ref, offset_ref, prior_ref, summary_ref, kernel_ref,
    out_ref, lhs, rhs, prior, score_a, score_b, top, peak, first, second, owner, start, row_sem, col_sem,
):
    blocks = cols // BLOCK
    per_tile = tile_rows // GROUP
    sizes = [1 << k for k in reversed(range(per_tile.bit_length()))]
    stride = 2 * tiles + 1

    def row_copies(act):
        for t in range(tiles):
            count = lax.div(live_ref[t] + (GROUP - 1), GROUP)
            base = start[t]
            for k, size in enumerate(sizes):
                done = lax.bitwise_and(count, ~(2 * size - 1))

                @pl.when(lax.bitwise_and(count, size) != 0)
                def _():
                    copy = pltpu.make_async_copy(
                        summary_ref.at[pl.ds(pl.multiple_of(t * tile_rows + done * GROUP, GROUP), size * GROUP)],
                        lhs.at[pl.ds(pl.multiple_of((base + done) * GROUP, GROUP), size * GROUP)],
                        row_sem.at[t, k],
                    )
                    act(copy)

    def col_copy(n):
        return pltpu.make_async_copy(kernel_ref.at[:, pl.ds(n * BLOCK, BLOCK)], rhs.at[n], col_sem.at[n])

    total = jnp.int32(0)
    for t in range(tiles):
        start[t] = total
        total = total + lax.div(live_ref[t] + (GROUP - 1), GROUP)
    row_copies(lambda copy: copy.start())
    for n in range(blocks):
        col_copy(n).start()

    chunk_groups = CHUNK // GROUP
    chunks = lax.div(total + (chunk_groups - 1), chunk_groups)
    for t in range(tiles):
        count = lax.div(live_ref[t] + (GROUP - 1), GROUP)

        def mark(j, carry):
            owner[start[t] + j] = t
            return carry

        lax.fori_loop(0, count, mark, 0)
        row_at = lax.broadcasted_iota(jnp.int32, (1, tile_rows), 1)
        held = jnp.where(row_at < live_ref[t], prior_ref[t : t + 1, :], jnp.float32(DEAD))
        spread = jnp.broadcast_to(held, (LANES, tile_rows)).T
        prior[pl.ds(pl.multiple_of(start[t] * GROUP, GROUP), tile_rows), :] = spread
    for j in range(chunk_groups):
        owner[total + j] = tiles

    top[...] = jnp.full(top.shape, NEG, jnp.float32)
    first[...] = jnp.zeros(first.shape, jnp.float32)
    second[...] = jnp.zeros(second.shape, jnp.float32)
    peak[...] = jnp.zeros(peak.shape, jnp.float32)
    row_copies(lambda copy: copy.wait())

    def slot_of(tile, w):
        return pl.ds(pl.multiple_of(tile * 8 + w * (8 * tiles + 8), 8), 8)

    def products(n, c, score):
        row = pl.multiple_of(c * CHUNK, CHUNK)
        rows = lhs[pl.ds(row, CHUNK), :]
        for h in range(BLOCK // 256):
            part = jnp.dot(rows, rhs[n, :, h * 256 : (h + 1) * 256], preferred_element_type=jnp.float32)
            for g in range(chunk_groups):
                at = pl.ds(pl.multiple_of(row + g * GROUP, GROUP), GROUP)
                held = prior[at, :]
                for w in range(256 // LANES):
                    lane = pl.ds(h * 256 + w * LANES, LANES)
                    slot = slot_of(owner[c * chunk_groups + g], h * 2 + w)
                    value = part[g * GROUP : (g + 1) * GROUP, w * LANES : (w + 1) * LANES] - held
                    score[at, lane] = value
                    top[slot, :] = jnp.maximum(top[slot, :], jnp.maximum(value[:8], value[8:]))

    def sums(c, score):
        row = pl.multiple_of(c * CHUNK, CHUNK)
        for g in range(chunk_groups):
            at = pl.ds(pl.multiple_of(row + g * GROUP, GROUP), GROUP)
            tile = owner[c * chunk_groups + g]
            for w in range(BLOCK // LANES):
                slot = slot_of(tile, w)
                level = peak[pl.ds(tile + w * (tiles + 8), 8, stride=0), :]
                value = score[at, pl.ds(w * LANES, LANES)]
                low, high = jnp.exp(value[:8] - level), jnp.exp(value[8:] - level)
                first[slot, :] = first[slot, :] + (low + high)
                second[slot, :] = second[slot, :] + (low * low + high * high)

    def fold(ref, half, w, join):
        parts = [ref[pl.ds(w * (8 * tiles + 8) + half * 64 + i, 8, stride=8), :] for i in range(8)]
        while len(parts) > 1:
            parts = [join(a, b) for a, b in zip(parts[::2], parts[1::2])]
        return parts[0]

    def close_top():
        for half in range(tiles // 8):
            for w in range(BLOCK // LANES):
                peak[pl.ds(w * (tiles + 8) + half * 8, 8), :] = fold(top, half, w, jnp.maximum)
        top[...] = jnp.full(top.shape, NEG, jnp.float32)

    def close_sums(n):
        for half in range(tiles // 8):
            for w in range(BLOCK // LANES):
                one = fold(first, half, w, jnp.add)
                two = fold(second, half, w, jnp.add)
                level = peak[pl.ds(w * (tiles + 8) + half * 8, 8), :]
                shift = offset_ref[:, pl.ds(pl.multiple_of(n * BLOCK + w * LANES, LANES), LANES)]
                base = (n * (BLOCK // LANES) + w) * stride + half * 8
                out_ref[pl.ds(base, 8), :] = level + jnp.log(one) + shift
                out_ref[pl.ds(base + tiles, 8), :] = two / (one * one)
        first[...] = jnp.zeros(first.shape, jnp.float32)
        second[...] = jnp.zeros(second.shape, jnp.float32)

    def each_chunk(work):
        def step(c, carry):
            work(c)
            return carry

        lax.fori_loop(0, chunks, step, 0)

    col_copy(0).wait()
    each_chunk(lambda c: products(0, c, score_a))

    def step(n, now, before):
        close_top()
        col_copy(n).wait()

        def work(c):
            products(n, c, now)
            sums(c, before)

        each_chunk(work)
        close_sums(n - 1)

    def pair(i, carry):
        step(2 * i + 1, score_b, score_a)

        @pl.when(i < blocks // 2 - 1)
        def _():
            step(2 * i + 2, score_a, score_b)

        return carry

    lax.fori_loop(0, blocks // 2, pair, 0)
    close_top()
    each_chunk(lambda c: sums(c, score_b))
    close_sums(blocks - 1)

    lane_at = lax.broadcasted_iota(jnp.int32, (1, LANES), 1)
    facts = jnp.zeros((1, LANES), jnp.float32)
    for t in range(tiles):
        facts = jnp.where(lane_at == t, event_ref[t].astype(jnp.float32), facts)
        facts = jnp.where(lane_at == tiles + t, live_ref[t].astype(jnp.float32), facts)
    for d in range(cols // LANES):
        out_ref[d * stride + 2 * tiles : d * stride + 2 * tiles + 1, :] = facts


def tile_stats(summary, kernel, grid_offset, log_prior, tile_event, tile_live):
    rows, depth = summary.shape
    cols = kernel.shape[1]
    tiles = tile_event.shape[0]
    tile_rows = rows // tiles
    stride = 2 * tiles + 1
    smem = pl.BlockSpec(memory_space=pltpu.SMEM)
    vmem = pl.BlockSpec(memory_space=pltpu.VMEM)
    hbm = pl.BlockSpec(memory_space=pl.ANY)
    f32 = jnp.float32
    return pl.pallas_call(
        functools.partial(stats_kernel, tiles, tile_rows, depth, cols),
        out_shape=jax.ShapeDtypeStruct((cols // LANES * stride, LANES), f32),
        in_specs=[smem, smem, vmem, vmem, hbm, hbm],
        out_specs=vmem,
        scratch_shapes=[
            pltpu.VMEM((rows + CHUNK, depth), jnp.bfloat16),
            pltpu.VMEM((cols // BLOCK, depth, BLOCK), jnp.bfloat16),
            pltpu.VMEM((rows + CHUNK, LANES), f32),
            pltpu.VMEM((rows + CHUNK, BLOCK), f32),
            pltpu.VMEM((rows + CHUNK, BLOCK), f32),
            pltpu.VMEM((BLOCK // LANES * (8 * tiles + 8), LANES), f32),
            pltpu.VMEM((BLOCK // LANES * (tiles + 8), LANES), f32),
            pltpu.VMEM((BLOCK // LANES * (8 * tiles + 8), LANES), f32),
            pltpu.VMEM((BLOCK // LANES * (8 * tiles + 8), LANES), f32),
            pltpu.SMEM((rows // GROUP + CHUNK // GROUP,), jnp.int32),
            pltpu.SMEM((tiles,), jnp.int32),
            pltpu.SemaphoreType.DMA((tiles, (tile_rows // GROUP).bit_length())),
            pltpu.SemaphoreType.DMA((cols // BLOCK,)),
        ],
        compiler_params=pltpu.CompilerParams(vmem_limit_bytes=48 << 20),
    )(
        tile_event, tile_live, grid_offset.reshape(1, cols), log_prior.reshape(tiles, tile_rows), summary, kernel,
    )


def split3(x):
    high = x.astype(jnp.bfloat16)
    rest = x - high.astype(jnp.float32)
    middle = rest.astype(jnp.bfloat16)
    low = (rest - middle.astype(jnp.float32)).astype(jnp.bfloat16)
    return high, middle, low


def merge_kernel(devices, tiles, got_ref, out_ref, level, event, ratio, live, peak_of, peak, kept):
    stride = 2 * tiles + 1
    total = devices * tiles
    facts = got_ref[pl.ds(2 * tiles, devices, stride=stride), :]
    for i in range(tiles):
        at = slice(i * devices, (i + 1) * devices)
        level[at, :] = got_ref[pl.ds(i, devices, stride=stride), :]
        ratio[at, :] = got_ref[pl.ds(tiles + i, devices, stride=stride), :]
        event[at, :] = jnp.broadcast_to(facts[:, i : i + 1], (devices, LANES))
        live[at, :] = jnp.broadcast_to(facts[:, tiles + i : tiles + i + 1], (devices, LANES))

    def find(e, carry):
        name = e.astype(jnp.float32)
        parts = [jnp.full((8, LANES), NEG, jnp.float32) for _ in range(4)]
        for v in range(total // 8):
            at = slice(v * 8, v * 8 + 8)
            parts[v % 4] = jnp.maximum(
                parts[v % 4], jnp.where(event[at, :] == name, level[at, :], jnp.float32(NEG))
            )
        best = jnp.maximum(jnp.maximum(parts[0], parts[1]), jnp.maximum(parts[2], parts[3]))
        best = jnp.max(best, axis=0, keepdims=True)
        peak[pl.ds(e, 1), :] = best
        wide = jnp.broadcast_to(best, (8, LANES))
        for v in range(total // 8):
            at = slice(v * 8, v * 8 + 8)
            peak_of[at, :] = jnp.where(event[at, :] == name, wide, peak_of[at, :])
        return carry

    lax.fori_loop(0, EVENTS, find, 0)
    one = jnp.exp(level[...] - peak_of[...])
    two = ratio[...] * one * one
    lanes = lax.broadcasted_iota(jnp.int32, (total, LANES), 1).astype(jnp.float32)
    chosen = jnp.where(event[...] == lanes, jnp.float32(1), jnp.float32(0)).astype(jnp.bfloat16)
    right = jnp.concatenate(split3(one) + split3(two) + (live[...].astype(jnp.bfloat16),), axis=1)
    sums = lax.dot_general(chosen, right, (((0,), (0,)), ((), ())), preferred_element_type=jnp.float32)
    part = [sums[:EVENTS, k * LANES : (k + 1) * LANES] for k in range(7)]
    first = part[0] + part[1] + part[2]
    second = part[3] + part[4] + part[5]
    count = part[6]
    evidence = peak[...] + jnp.log(first) - jnp.log(count)
    kept[:EVENTS, :] = evidence
    kept[EVENTS:, :] = first * first / (second * count)
    own = EVENTS // devices
    out_stride = 2 * own + 1
    for k in range(own):
        out_ref[pl.ds(k, devices, stride=out_stride), :] = kept[pl.ds(k, devices, stride=own), :]
        out_ref[pl.ds(own + k, devices, stride=out_stride), :] = kept[pl.ds(EVENTS + k, devices, stride=own), :]
    loglik = jnp.sum(evidence, axis=0, keepdims=True) / jnp.float32(EVENTS)
    out_ref[pl.ds(2 * own, devices, stride=out_stride), :] = jnp.broadcast_to(loglik, (devices, LANES))


def merge(got, devices, tiles):
    total = devices * tiles
    f32 = jnp.float32
    vmem = pl.BlockSpec(memory_space=pltpu.VMEM)
    return pl.pallas_call(
        functools.partial(merge_kernel, devices, tiles),
        out_shape=jax.ShapeDtypeStruct((devices * (2 * (EVENTS // devices) + 1), LANES), f32),
        in_specs=[vmem],
        out_specs=vmem,
        scratch_shapes=[pltpu.VMEM((total, LANES), f32)] * 5
        + [pltpu.VMEM((EVENTS, LANES), f32), pltpu.VMEM((2 * EVENTS, LANES), f32)],
    )(got)


def last_kernel(devices, own, got_ref, evidence_ref, ess_ref, posterior_ref):
    stride = 2 * own + 1
    for d in range(devices):
        lane = slice(d * LANES, (d + 1) * LANES)
        evidence_ref[:, lane] = got_ref[d * stride : d * stride + own, :]
        ess_ref[:, lane] = got_ref[d * stride + own : d * stride + 2 * own, :]
    loglik = got_ref[pl.ds(2 * own, devices, stride=stride), :]
    top = jnp.max(jnp.max(loglik, axis=0, keepdims=True), axis=1, keepdims=True)
    mass = jnp.exp(loglik - top)
    mass = jnp.sum(jnp.sum(mass, axis=0, keepdims=True), axis=1, keepdims=True)
    posterior_ref[...] = loglik - (top + jnp.log(mass))


def last(got, devices, own):
    f32 = jnp.float32
    vmem = pl.BlockSpec(memory_space=pltpu.VMEM)
    cols = devices * LANES
    return pl.pallas_call(
        functools.partial(last_kernel, devices, own),
        out_shape=(
            jax.ShapeDtypeStruct((own, cols), f32),
            jax.ShapeDtypeStruct((own, cols), f32),
            jax.ShapeDtypeStruct((devices, LANES), f32),
        ),
        in_specs=[vmem],
        out_specs=(vmem, vmem, vmem),
    )(got)


def exchange(x, devices):
    width = x.shape[0] // devices * LANES
    got = lax.all_to_all(x.reshape(devices, 1, width), "samp", split_axis=0, concat_axis=0, tiled=True)
    return got.reshape(x.shape)


def column_body(devices, summary, kernel, grid_offset, log_prior, tile_event, tile_live):
    tiles = tile_event.shape[0]
    own = EVENTS // devices
    sent = tile_stats(summary, kernel, grid_offset, log_prior, tile_event, tile_live)
    merged = merge(exchange(sent, devices), devices, tiles)
    evidence, ess, posterior = last(exchange(merged, devices), devices, own)
    return evidence, ess, posterior.reshape(-1)


def row_body(summary, kernel, grid_offset, log_prior, tile_event, tile_live):
    row_count = summary.shape[0]
    grid_cols = kernel.shape[1]
    tile_count = tile_event.shape[0]
    tile_rows = row_count // tile_count
    scores = jnp.dot(summary, kernel, preferred_element_type=jnp.float32)
    scores = scores + grid_offset[None, :] - log_prior[:, None]
    scores = scores.reshape(tile_count, tile_rows, grid_cols)
    is_live = lax.broadcasted_iota(jnp.int32, (tile_count, tile_rows), 1) < tile_live[:, None]
    masked = jnp.where(is_live[:, :, None], scores, jnp.float32(-1e30))
    tile_max = jnp.max(masked, axis=1)
    shifted = jnp.exp(masked - tile_max[:, None, :])
    tile_first = jnp.sum(shifted, axis=1)
    tile_second = jnp.sum(shifted * shifted, axis=1)
    member = tile_event[None, :] == lax.broadcasted_iota(jnp.int32, (EVENTS, tile_count), 0)
    local_peak = jnp.max(
        jnp.where(member[:, :, None], tile_max[None, :, :], jnp.float32(-1e30)), axis=1
    )
    live_count = jnp.sum(jnp.where(member, tile_live[None, :], 0), axis=1).astype(jnp.float32)
    factor = jnp.exp(tile_max - local_peak[tile_event])
    member_float = member.astype(jnp.float32)
    local_first = jnp.dot(member_float, tile_first * factor, precision=lax.Precision.HIGHEST)
    local_second = jnp.dot(
        member_float, tile_second * factor * factor, precision=lax.Precision.HIGHEST
    )
    got_peak, got_first, got_second, got_count = (
        lax.all_to_all(local_peak[:, None, :], "samp", split_axis=0, concat_axis=1, tiled=True),
        lax.all_to_all(local_first[:, None, :], "samp", split_axis=0, concat_axis=1, tiled=True),
        lax.all_to_all(local_second[:, None, :], "samp", split_axis=0, concat_axis=1, tiled=True),
        lax.all_to_all(live_count[:, None, None], "samp", split_axis=0, concat_axis=1, tiled=True),
    )
    event_peak = jnp.max(got_peak, axis=1)
    rescale = jnp.exp(got_peak - event_peak[:, None, :])
    first_sum = jnp.sum(got_first * rescale, axis=1)
    second_sum = jnp.sum(got_second * rescale * rescale, axis=1)
    total_live = jnp.sum(got_count[:, :, 0], axis=1)
    log_evidence = event_peak + jnp.log(first_sum) - jnp.log(total_live)[:, None]
    ess_fraction = first_sum * first_sum / (second_sum * total_live[:, None])
    loglik = lax.psum(jnp.sum(log_evidence, axis=0), "samp") / jnp.float32(EVENTS)
    local_top = jnp.max(loglik)
    grid_top = lax.pmax(local_top, "grid")
    grid_mass = lax.psum(jnp.sum(jnp.exp(loglik - grid_top)), "grid")
    log_posterior = loglik - (grid_top + jnp.log(grid_mass))
    return (log_evidence, ess_fraction, log_posterior)


def solution(mesh):
    in_specs = (P("samp", None), P(None, "grid"), P("grid"), P("samp"), P("samp"), P("samp"))
    out_specs = (P("samp", "grid"), P("samp", "grid"), P("grid"))
    devices = mesh.shape["samp"]

    def body(summary, kernel, *rest):
        tile_rows = summary.shape[0] // rest[2].shape[0]
        whole_lanes = kernel.shape[1] == devices * LANES and tile_rows == LANES
        if mesh.shape["grid"] == 1 and whole_lanes:
            return column_body(devices, summary, kernel, *rest)
        return row_body(summary, kernel, *rest)

    return jax.shard_map(body, mesh=mesh, in_specs=in_specs, out_specs=out_specs, check_vma=False)
```

```python
import functools

import jax
import jax.numpy as jnp
from jax import lax
from jax.experimental import pallas as pl
from jax.experimental.pallas import tpu as pltpu
from jax.sharding import PartitionSpec as P

EVENTS = 64
LANES = 128
GROUP = 16
CHUNK = 256
BLOCK = 1024
NEG = -1e30
DEAD = 1e30


def stats_kernel(
    tiles, tile_rows, depth, cols, event_hbm, live_hbm, offset_hbm, prior_hbm, summary_ref, kernel_ref,
    out_ref, lhs, rhs, prior, score_a, score_b, top, peak, held_sums, offset_ref, prior_ref,
    event_ref, live_ref, owner, fresh, start, row_sem, col_sem, fact_sem,
):
    blocks = cols // BLOCK
    per_tile = tile_rows // GROUP
    sizes = [1 << k for k in reversed(range(per_tile.bit_length()))]
    stride = 2 * tiles + 1
    lanes = BLOCK // LANES
    span = 8 * tiles + 8
    peak_span = tiles + 8
    parts = lanes // 2
    chunk_groups = CHUNK // GROUP

    facts = [
        pltpu.make_async_copy(source, target, fact_sem.at[k])
        for k, (source, target) in enumerate(
            ((live_hbm, live_ref), (event_hbm, event_ref), (prior_hbm, prior_ref), (offset_hbm, offset_ref))
        )
    ]
    for copy in facts:
        copy.start()

    def col_copy(n):
        return pltpu.make_async_copy(kernel_ref.at[:, pl.ds(n * BLOCK, BLOCK)], rhs.at[n], col_sem.at[n])

    col_copy(0).start()

    def row_copies(act):
        for t in range(tiles):
            count = lax.div(live_ref[t] + (GROUP - 1), GROUP)
            base = start[t]
            for k, size in enumerate(sizes):
                done = lax.bitwise_and(count, ~(2 * size - 1))

                @pl.when(lax.bitwise_and(count, size) != 0)
                def _():
                    copy = pltpu.make_async_copy(
                        summary_ref.at[pl.ds(pl.multiple_of(t * tile_rows + done * GROUP, GROUP), size * GROUP)],
                        lhs.at[pl.ds(pl.multiple_of((base + done) * GROUP, GROUP), size * GROUP)],
                        row_sem.at[t, k],
                    )
                    act(copy)

    facts[0].wait()
    total = jnp.int32(0)
    for t in range(tiles):
        start[t] = total
        total = total + lax.div(live_ref[t] + (GROUP - 1), GROUP)
    row_copies(lambda copy: copy.start())
    for n in range(1, blocks):
        col_copy(n).start()
    for copy in facts[1:]:
        copy.wait()

    chunks = lax.div(total + (chunk_groups - 1), chunk_groups)
    for t in range(tiles):
        count = lax.div(live_ref[t] + (GROUP - 1), GROUP)

        def mark(j, carry):
            owner[start[t] + j] = t
            fresh[start[t] + j] = jnp.where(j == 0, jnp.float32(0), jnp.float32(1))
            return carry

        lax.fori_loop(0, count, mark, 0)
        row_at = lax.broadcasted_iota(jnp.int32, (1, tile_rows), 1)
        held = jnp.where(row_at < live_ref[t], prior_ref[t : t + 1, :], jnp.float32(DEAD))
        spread = jnp.broadcast_to(held, (LANES, tile_rows)).T
        prior[pl.ds(pl.multiple_of(start[t] * GROUP, GROUP), tile_rows), :] = spread
    for j in range(chunk_groups):
        owner[total + j] = tiles
        fresh[total + j] = jnp.float32(0)

    top[...] = jnp.zeros(top.shape, jnp.float32)
    held_sums[...] = jnp.zeros(held_sums.shape, jnp.float32)
    peak[...] = jnp.zeros(peak.shape, jnp.float32)
    row_copies(lambda copy: copy.wait())

    def rows_at(c, g):
        return pl.ds(pl.multiple_of(c * CHUNK, CHUNK) + g * GROUP, GROUP)

    def products(n, c, score, h):
        rows = lhs[pl.ds(pl.multiple_of(c * CHUNK, CHUNK), CHUNK), :]
        part = jnp.dot(rows, rhs[n, :, h * 256 : (h + 1) * 256], preferred_element_type=jnp.float32)
        base = pl.multiple_of(owner[c * chunk_groups] * 8, 8)
        held = [top[pl.ds(base + (h * 2 + w) * span, 8), :] for w in range(2)]
        for g in range(chunk_groups):
            base = pl.multiple_of(owner[c * chunk_groups + g] * 8, 8)
            reset = fresh[c * chunk_groups + g] * jnp.float32(DEAD) - jnp.float32(DEAD)
            cost = prior[rows_at(c, g), :]
            for w in range(2):
                lane = h * 2 + w
                value = part[g * GROUP : (g + 1) * GROUP, w * LANES : (w + 1) * LANES] - cost
                score[rows_at(c, g), lane * LANES : (lane + 1) * LANES] = value
                held[w] = jnp.maximum(held[w] + reset, jnp.maximum(value[:8], value[8:]))
                top[pl.ds(base + lane * span, 8), :] = held[w]

    def sums_open(c):
        base = pl.multiple_of(owner[c * chunk_groups] * 8, 8)
        return [
            [held_sums[pl.ds(base + (k * lanes + lane) * span, 8), :] for lane in range(lanes)] for k in range(2)
        ]

    def sums(c, score, part, held):
        one, two = held
        for g in range(part * chunk_groups // parts, (part + 1) * chunk_groups // parts):
            tile = owner[c * chunk_groups + g]
            base = pl.multiple_of(tile * 8, 8)
            keep = fresh[c * chunk_groups + g]
            for lane in range(lanes):
                level = peak[pl.ds(tile + lane * peak_span, 8, stride=0), :]
                value = score[rows_at(c, g), lane * LANES : (lane + 1) * LANES]
                low, high = jnp.exp(value[:8] - level), jnp.exp(value[8:] - level)
                one[lane] = one[lane] * keep + (low + high)
                two[lane] = two[lane] * keep + (low * low + high * high)
                held_sums[pl.ds(base + lane * span, 8), :] = one[lane]
                held_sums[pl.ds(base + (lanes + lane) * span, 8), :] = two[lane]

    def fold(ref, half, w, join):
        kept = [ref[pl.ds(w * span + half * 64 + i, 8, stride=8), :] for i in range(8)]
        while len(kept) > 1:
            kept = [join(a, b) for a, b in zip(kept[::2], kept[1::2])]
        return kept[0]

    def close_top():
        for half in range(tiles // 8):
            for w in range(lanes):
                peak[pl.ds(w * peak_span + half * 8, 8), :] = fold(top, half, w, jnp.maximum)

    def close_sums(n):
        for half in range(tiles // 8):
            for w in range(lanes):
                one = fold(held_sums, half, w, jnp.add)
                two = fold(held_sums, half, lanes + w, jnp.add)
                level = peak[pl.ds(w * peak_span + half * 8, 8), :]
                shift = offset_ref[:, pl.ds(pl.multiple_of(n * BLOCK + w * LANES, LANES), LANES)]
                base = (n * lanes + w) * stride + half * 8
                out_ref[pl.ds(base, 8), :] = level + jnp.log(one) + shift
                out_ref[pl.ds(base + tiles, 8), :] = two / (one * one)

    def each_chunk(work):
        def step(c, carry):
            work(c)
            return carry

        lax.fori_loop(0, chunks, step, 0)

    def only_products(c):
        for h in range(lanes // 2):
            products(0, c, score_a, h)

    def only_sums(c):
        held = sums_open(c)
        for h in range(parts):
            sums(c, score_b, h, held)

    col_copy(0).wait()
    each_chunk(only_products)

    def step(n, now, before):
        close_top()
        col_copy(n).wait()

        def work(c):
            held = sums_open(c)
            for h in range(parts):
                sums(c, before, h, held)
                products(n, c, now, h)

        each_chunk(work)
        close_sums(n - 1)

    def pair(i, carry):
        step(2 * i + 1, score_b, score_a)

        @pl.when(i < blocks // 2 - 1)
        def _():
            step(2 * i + 2, score_a, score_b)

        return carry

    lax.fori_loop(0, blocks // 2, pair, 0)
    close_top()
    each_chunk(only_sums)
    close_sums(blocks - 1)

    lane_at = lax.broadcasted_iota(jnp.int32, (1, LANES), 1)
    facts = jnp.zeros((1, LANES), jnp.float32)
    for t in range(tiles):
        facts = jnp.where(lane_at == t, event_ref[t].astype(jnp.float32), facts)
        facts = jnp.where(lane_at == tiles + t, live_ref[t].astype(jnp.float32), facts)
    for d in range(cols // LANES):
        out_ref[d * stride + 2 * tiles : d * stride + 2 * tiles + 1, :] = facts


def tile_stats(summary, kernel, grid_offset, log_prior, tile_event, tile_live):
    rows, depth = summary.shape
    cols = kernel.shape[1]
    tiles = tile_event.shape[0]
    tile_rows = rows // tiles
    stride = 2 * tiles + 1
    hbm = pl.BlockSpec(memory_space=pltpu.HBM)
    f32 = jnp.float32
    lanes = BLOCK // LANES
    groups = (rows + CHUNK) // GROUP
    return pl.pallas_call(
        functools.partial(stats_kernel, tiles, tile_rows, depth, cols),
        out_shape=jax.ShapeDtypeStruct((cols // LANES * stride, LANES), f32),
        in_specs=[hbm] * 6,
        out_specs=pl.BlockSpec(memory_space=pltpu.VMEM),
        scratch_shapes=[
            pltpu.VMEM((rows + CHUNK, depth), jnp.bfloat16),
            pltpu.VMEM((cols // BLOCK, depth, BLOCK), jnp.bfloat16),
            pltpu.VMEM((rows + CHUNK, LANES), f32),
            pltpu.VMEM((rows + CHUNK, BLOCK), f32),
            pltpu.VMEM((rows + CHUNK, BLOCK), f32),
            pltpu.VMEM((lanes * (8 * tiles + 8), LANES), f32),
            pltpu.VMEM((lanes * (tiles + 8), LANES), f32),
            pltpu.VMEM((2 * lanes * (8 * tiles + 8), LANES), f32),
            pltpu.VMEM((1, cols), f32),
            pltpu.VMEM((tiles, tile_rows), f32),
            pltpu.SMEM((tiles,), jnp.int32),
            pltpu.SMEM((tiles,), jnp.int32),
            pltpu.SMEM((groups,), jnp.int32),
            pltpu.SMEM((groups,), f32),
            pltpu.SMEM((tiles,), jnp.int32),
            pltpu.SemaphoreType.DMA((tiles, (tile_rows // GROUP).bit_length())),
            pltpu.SemaphoreType.DMA((cols // BLOCK,)),
            pltpu.SemaphoreType.DMA((4,)),
        ],
        compiler_params=pltpu.CompilerParams(vmem_limit_bytes=56 << 20),
    )(
        tile_event, tile_live, grid_offset.reshape(1, cols), log_prior.reshape(tiles, tile_rows), summary, kernel,
    )


def split3(x):
    high = x.astype(jnp.bfloat16)
    rest = x - high.astype(jnp.float32)
    middle = rest.astype(jnp.bfloat16)
    low = (rest - middle.astype(jnp.float32)).astype(jnp.bfloat16)
    return high, middle, low


def merge_kernel(devices, tiles, got_ref, out_ref, level, event, ratio, live, peak_of, peak, kept):
    stride = 2 * tiles + 1
    total = devices * tiles
    facts = got_ref[pl.ds(2 * tiles, devices, stride=stride), :]
    for i in range(tiles):
        at = slice(i * devices, (i + 1) * devices)
        level[at, :] = got_ref[pl.ds(i, devices, stride=stride), :]
        ratio[at, :] = got_ref[pl.ds(tiles + i, devices, stride=stride), :]
        event[at, :] = jnp.broadcast_to(facts[:, i : i + 1], (devices, LANES))
        live[at, :] = jnp.broadcast_to(facts[:, tiles + i : tiles + i + 1], (devices, LANES))

    def find(e, carry):
        name = e.astype(jnp.float32)
        parts = [jnp.full((8, LANES), NEG, jnp.float32) for _ in range(4)]
        for v in range(total // 8):
            at = slice(v * 8, v * 8 + 8)
            parts[v % 4] = jnp.maximum(
                parts[v % 4], jnp.where(event[at, :] == name, level[at, :], jnp.float32(NEG))
            )
        best = jnp.maximum(jnp.maximum(parts[0], parts[1]), jnp.maximum(parts[2], parts[3]))
        best = jnp.max(best, axis=0, keepdims=True)
        peak[pl.ds(e, 1), :] = best
        wide = jnp.broadcast_to(best, (8, LANES))
        for v in range(total // 8):
            at = slice(v * 8, v * 8 + 8)
            peak_of[at, :] = jnp.where(event[at, :] == name, wide, peak_of[at, :])
        return carry

    lax.fori_loop(0, EVENTS, find, 0)
    one = jnp.exp(level[...] - peak_of[...])
    two = ratio[...] * one * one
    lanes = lax.broadcasted_iota(jnp.int32, (total, LANES), 1).astype(jnp.float32)
    chosen = jnp.where(event[...] == lanes, jnp.float32(1), jnp.float32(0)).astype(jnp.bfloat16)
    right = jnp.concatenate(split3(one) + split3(two) + (live[...].astype(jnp.bfloat16),), axis=1)
    sums = lax.dot_general(chosen, right, (((0,), (0,)), ((), ())), preferred_element_type=jnp.float32)
    part = [sums[:EVENTS, k * LANES : (k + 1) * LANES] for k in range(7)]
    first = part[0] + part[1] + part[2]
    second = part[3] + part[4] + part[5]
    count = part[6]
    evidence = peak[...] + jnp.log(first) - jnp.log(count)
    kept[:EVENTS, :] = evidence
    kept[EVENTS:, :] = first * first / (second * count)
    own = EVENTS // devices
    out_stride = 2 * own + 1
    for k in range(own):
        out_ref[pl.ds(k, devices, stride=out_stride), :] = kept[pl.ds(k, devices, stride=own), :]
        out_ref[pl.ds(own + k, devices, stride=out_stride), :] = kept[pl.ds(EVENTS + k, devices, stride=own), :]
    loglik = jnp.sum(evidence, axis=0, keepdims=True) / jnp.float32(EVENTS)
    out_ref[pl.ds(2 * own, devices, stride=out_stride), :] = jnp.broadcast_to(loglik, (devices, LANES))


def merge(got, devices, tiles):
    total = devices * tiles
    f32 = jnp.float32
    vmem = pl.BlockSpec(memory_space=pltpu.VMEM)
    return pl.pallas_call(
        functools.partial(merge_kernel, devices, tiles),
        out_shape=jax.ShapeDtypeStruct((devices * (2 * (EVENTS // devices) + 1), LANES), f32),
        in_specs=[vmem],
        out_specs=vmem,
        scratch_shapes=[pltpu.VMEM((total, LANES), f32)] * 5
        + [pltpu.VMEM((EVENTS, LANES), f32), pltpu.VMEM((2 * EVENTS, LANES), f32)],
    )(got)


def last_kernel(devices, own, got_ref, evidence_ref, ess_ref, posterior_ref):
    stride = 2 * own + 1
    for d in range(devices):
        lane = slice(d * LANES, (d + 1) * LANES)
        evidence_ref[:, lane] = got_ref[d * stride : d * stride + own, :]
        ess_ref[:, lane] = got_ref[d * stride + own : d * stride + 2 * own, :]
    loglik = got_ref[pl.ds(2 * own, devices, stride=stride), :]
    top = jnp.max(jnp.max(loglik, axis=0, keepdims=True), axis=1, keepdims=True)
    mass = jnp.exp(loglik - top)
    mass = jnp.sum(jnp.sum(mass, axis=0, keepdims=True), axis=1, keepdims=True)
    posterior_ref[...] = loglik - (top + jnp.log(mass))


def last(got, devices, own):
    f32 = jnp.float32
    vmem = pl.BlockSpec(memory_space=pltpu.VMEM)
    cols = devices * LANES
    return pl.pallas_call(
        functools.partial(last_kernel, devices, own),
        out_shape=(
            jax.ShapeDtypeStruct((own, cols), f32),
            jax.ShapeDtypeStruct((own, cols), f32),
            jax.ShapeDtypeStruct((devices, LANES), f32),
        ),
        in_specs=[vmem],
        out_specs=(vmem, vmem, vmem),
    )(got)


def exchange(x, devices):
    width = x.shape[0] // devices * LANES
    got = lax.all_to_all(x.reshape(devices, 1, width), "samp", split_axis=0, concat_axis=0, tiled=True)
    return got.reshape(x.shape)


def column_body(devices, summary, kernel, grid_offset, log_prior, tile_event, tile_live):
    tiles = tile_event.shape[0]
    own = EVENTS // devices
    sent = tile_stats(summary, kernel, grid_offset, log_prior, tile_event, tile_live)
    merged = merge(exchange(sent, devices), devices, tiles)
    evidence, ess, posterior = last(exchange(merged, devices), devices, own)
    return evidence, ess, posterior.reshape(-1)


def row_body(summary, kernel, grid_offset, log_prior, tile_event, tile_live):
    row_count = summary.shape[0]
    grid_cols = kernel.shape[1]
    tile_count = tile_event.shape[0]
    tile_rows = row_count // tile_count
    scores = jnp.dot(summary, kernel, preferred_element_type=jnp.float32)
    scores = scores + grid_offset[None, :] - log_prior[:, None]
    scores = scores.reshape(tile_count, tile_rows, grid_cols)
    is_live = lax.broadcasted_iota(jnp.int32, (tile_count, tile_rows), 1) < tile_live[:, None]
    masked = jnp.where(is_live[:, :, None], scores, jnp.float32(-1e30))
    tile_max = jnp.max(masked, axis=1)
    shifted = jnp.exp(masked - tile_max[:, None, :])
    tile_first = jnp.sum(shifted, axis=1)
    tile_second = jnp.sum(shifted * shifted, axis=1)
    member = tile_event[None, :] == lax.broadcasted_iota(jnp.int32, (EVENTS, tile_count), 0)
    local_peak = jnp.max(
        jnp.where(member[:, :, None], tile_max[None, :, :], jnp.float32(-1e30)), axis=1
    )
    live_count = jnp.sum(jnp.where(member, tile_live[None, :], 0), axis=1).astype(jnp.float32)
    factor = jnp.exp(tile_max - local_peak[tile_event])
    member_float = member.astype(jnp.float32)
    local_first = jnp.dot(member_float, tile_first * factor, precision=lax.Precision.HIGHEST)
    local_second = jnp.dot(
        member_float, tile_second * factor * factor, precision=lax.Precision.HIGHEST
    )
    got_peak, got_first, got_second, got_count = (
        lax.all_to_all(local_peak[:, None, :], "samp", split_axis=0, concat_axis=1, tiled=True),
        lax.all_to_all(local_first[:, None, :], "samp", split_axis=0, concat_axis=1, tiled=True),
        lax.all_to_all(local_second[:, None, :], "samp", split_axis=0, concat_axis=1, tiled=True),
        lax.all_to_all(live_count[:, None, None], "samp", split_axis=0, concat_axis=1, tiled=True),
    )
    event_peak = jnp.max(got_peak, axis=1)
    rescale = jnp.exp(got_peak - event_peak[:, None, :])
    first_sum = jnp.sum(got_first * rescale, axis=1)
    second_sum = jnp.sum(got_second * rescale * rescale, axis=1)
    total_live = jnp.sum(got_count[:, :, 0], axis=1)
    log_evidence = event_peak + jnp.log(first_sum) - jnp.log(total_live)[:, None]
    ess_fraction = first_sum * first_sum / (second_sum * total_live[:, None])
    loglik = lax.psum(jnp.sum(log_evidence, axis=0), "samp") / jnp.float32(EVENTS)
    local_top = jnp.max(loglik)
    grid_top = lax.pmax(local_top, "grid")
    grid_mass = lax.psum(jnp.sum(jnp.exp(loglik - grid_top)), "grid")
    log_posterior = loglik - (grid_top + jnp.log(grid_mass))
    return (log_evidence, ess_fraction, log_posterior)


def solution(mesh):
    in_specs = (P("samp", None), P(None, "grid"), P("grid"), P("samp"), P("samp"), P("samp"))
    out_specs = (P("samp", "grid"), P("samp", "grid"), P("grid"))
    devices = mesh.shape["samp"]

    def body(summary, kernel, *rest):
        tile_rows = summary.shape[0] // rest[2].shape[0]
        whole_lanes = kernel.shape[1] == devices * LANES and tile_rows == LANES
        if mesh.shape["grid"] == 1 and whole_lanes:
            return column_body(devices, summary, kernel, *rest)
        return row_body(summary, kernel, *rest)

    return jax.shard_map(body, mesh=mesh, in_specs=in_specs, out_specs=out_specs, check_vma=False)
```

```python
import functools

import jax
import jax.numpy as jnp
from jax import lax
from jax.experimental import pallas as pl
from jax.experimental.pallas import tpu as pltpu
from jax.sharding import PartitionSpec as P

EVENTS = 64
LANES = 128
HALF = 64
GROUP = 16
CHUNK = 256
BLOCK = 1024
NEG = -1e30
DEAD = 1e30


def stats_kernel(
    tiles, tile_rows, cols, column, facts_row, event_hbm, live_hbm, offset_hbm, prior_hbm, summary_ref, kernel_ref,
    out_ref, lhs, rhs, prior, score_a, score_b, top, peak, held_sums, offset_ref, prior_ref,
    event_ref, live_ref, owner, fresh, start, row_sem, col_sem, fact_sem,
):
    blocks = cols // BLOCK
    per_tile = tile_rows // GROUP
    sizes = [1 << k for k in reversed(range(per_tile.bit_length()))]
    half_tiles = tiles // 2
    stride = tiles + facts_row
    lanes = BLOCK // LANES
    span = 8 * tiles + 8
    peak_span = tiles + 8
    parts = lanes // 2
    chunk_groups = CHUNK // GROUP

    facts = [
        pltpu.make_async_copy(source, target, fact_sem.at[k])
        for k, (source, target) in enumerate(
            ((live_hbm, live_ref), (event_hbm, event_ref), (prior_hbm, prior_ref), (offset_hbm, offset_ref))
        )
    ]
    for copy in facts:
        copy.start()

    def col_copy(n):
        return pltpu.make_async_copy(kernel_ref.at[:, pl.ds(column + n * BLOCK, BLOCK)], rhs.at[n], col_sem.at[n])

    col_copy(0).start()

    def row_copies(act):
        for t in range(tiles):
            count = lax.div(live_ref[t] + (GROUP - 1), GROUP)
            base = start[t]
            for k, size in enumerate(sizes):
                done = lax.bitwise_and(count, ~(2 * size - 1))

                @pl.when(lax.bitwise_and(count, size) != 0)
                def _():
                    copy = pltpu.make_async_copy(
                        summary_ref.at[pl.ds(pl.multiple_of(t * tile_rows + done * GROUP, GROUP), size * GROUP)],
                        lhs.at[pl.ds(pl.multiple_of((base + done) * GROUP, GROUP), size * GROUP)],
                        row_sem.at[t, k],
                    )
                    act(copy)

    facts[0].wait()
    total = jnp.int32(0)
    for t in range(tiles):
        start[t] = total
        total = total + lax.div(live_ref[t] + (GROUP - 1), GROUP)
    row_copies(lambda copy: copy.start())
    for n in range(1, blocks):
        col_copy(n).start()
    for copy in facts[1:]:
        copy.wait()

    chunks = lax.div(total + (chunk_groups - 1), chunk_groups)
    for t in range(tiles):
        count = lax.div(live_ref[t] + (GROUP - 1), GROUP)

        def mark(j, carry):
            owner[start[t] + j] = t
            fresh[start[t] + j] = jnp.where(j == 0, jnp.float32(0), jnp.float32(1))
            return carry

        lax.fori_loop(0, count, mark, 0)
        row_at = lax.broadcasted_iota(jnp.int32, (1, tile_rows), 1)
        held = jnp.where(row_at < live_ref[t], prior_ref[t : t + 1, :], jnp.float32(DEAD))
        spread = jnp.broadcast_to(held, (LANES, tile_rows)).T
        prior[pl.ds(pl.multiple_of(start[t] * GROUP, GROUP), tile_rows), :] = spread
    for j in range(chunk_groups):
        owner[total + j] = tiles
        fresh[total + j] = jnp.float32(0)

    top[...] = jnp.zeros(top.shape, jnp.float32)
    held_sums[...] = jnp.zeros(held_sums.shape, jnp.float32)
    peak[...] = jnp.zeros(peak.shape, jnp.float32)
    row_copies(lambda copy: copy.wait())

    def rows_at(c, g):
        return pl.ds(pl.multiple_of(c * CHUNK, CHUNK) + g * GROUP, GROUP)

    def products(n, c, score, h):
        rows = lhs[pl.ds(pl.multiple_of(c * CHUNK, CHUNK), CHUNK), :]
        part = jnp.dot(rows, rhs[n, :, h * 256 : (h + 1) * 256], preferred_element_type=jnp.float32)
        base = pl.multiple_of(owner[c * chunk_groups] * 8, 8)
        held = [top[pl.ds(base + (h * 2 + w) * span, 8), :] for w in range(2)]
        for g in range(chunk_groups):
            base = pl.multiple_of(owner[c * chunk_groups + g] * 8, 8)
            reset = fresh[c * chunk_groups + g] * jnp.float32(DEAD) - jnp.float32(DEAD)
            cost = prior[rows_at(c, g), :]
            for w in range(2):
                lane = h * 2 + w
                value = part[g * GROUP : (g + 1) * GROUP, w * LANES : (w + 1) * LANES] - cost
                score[rows_at(c, g), lane * LANES : (lane + 1) * LANES] = value
                held[w] = jnp.maximum(held[w] + reset, jnp.maximum(value[:8], value[8:]))
                top[pl.ds(base + lane * span, 8), :] = held[w]

    def sums_open(c):
        base = pl.multiple_of(owner[c * chunk_groups] * 8, 8)
        return [
            [held_sums[pl.ds(base + (k * lanes + lane) * span, 8), :] for lane in range(lanes)] for k in range(2)
        ]

    def sums(c, score, part, held):
        one, two = held
        for g in range(part * chunk_groups // parts, (part + 1) * chunk_groups // parts):
            tile = owner[c * chunk_groups + g]
            base = pl.multiple_of(tile * 8, 8)
            keep = fresh[c * chunk_groups + g]
            for lane in range(lanes):
                level = peak[pl.ds(tile + lane * peak_span, 8, stride=0), :]
                value = score[rows_at(c, g), lane * LANES : (lane + 1) * LANES]
                low, high = jnp.exp(value[:8] - level), jnp.exp(value[8:] - level)
                one[lane] = one[lane] * keep + (low + high)
                two[lane] = two[lane] * keep + (low * low + high * high)
                held_sums[pl.ds(base + lane * span, 8), :] = one[lane]
                held_sums[pl.ds(base + (lanes + lane) * span, 8), :] = two[lane]

    def fold(ref, half, w, join):
        kept = [ref[pl.ds(w * span + half * 64 + i, 8, stride=8), :] for i in range(8)]
        while len(kept) > 1:
            kept = [join(a, b) for a, b in zip(kept[::2], kept[1::2])]
        return kept[0]

    def close_top():
        for half in range(tiles // 8):
            for w in range(lanes):
                peak[pl.ds(w * peak_span + half * 8, 8), :] = fold(top, half, w, jnp.maximum)

    left = lax.broadcasted_iota(jnp.int32, (8, LANES), 1) < HALF

    def close_sums(n):
        for w in range(lanes):
            shift = offset_ref[:, pl.ds(pl.multiple_of(column + n * BLOCK + w * LANES, LANES), LANES)]
            values = []
            for half in range(tiles // 8):
                one = fold(held_sums, half, w, jnp.add)
                two = fold(held_sums, half, lanes + w, jnp.add)
                level = peak[pl.ds(w * peak_span + half * 8, 8), :]
                values.append((level + jnp.log(one) + shift, two / (one * one)))
            for part in range(half_tiles // 8):
                for k in range(2):
                    low, high = values[part][k], values[half_tiles // 8 + part][k]
                    base = 2 * (n * lanes + w) * stride + k * half_tiles + part * 8
                    out_ref[pl.ds(base, 8), :] = jnp.where(left, low, pltpu.roll(high, HALF, 1))
                    out_ref[pl.ds(base + stride, 8), :] = jnp.where(left, pltpu.roll(low, HALF, 1), high)

    def each_chunk(work):
        def step(c, carry):
            work(c)
            return carry

        lax.fori_loop(0, chunks, step, 0)

    def only_products(c):
        for h in range(lanes // 2):
            products(0, c, score_a, h)

    def only_sums(c):
        held = sums_open(c)
        for h in range(parts):
            sums(c, score_b, h, held)

    col_copy(0).wait()
    each_chunk(only_products)

    def step(n, now, before):
        close_top()
        col_copy(n).wait()

        def work(c):
            held = sums_open(c)
            for h in range(parts):
                sums(c, before, h, held)
                products(n, c, now, h)

        each_chunk(work)
        close_sums(n - 1)

    def pair(i, carry):
        step(2 * i + 1, score_b, score_a)

        @pl.when(i < blocks // 2 - 1)
        def _():
            step(2 * i + 2, score_a, score_b)

        return carry

    lax.fori_loop(0, blocks // 2, pair, 0)
    close_top()
    each_chunk(only_sums)
    close_sums(blocks - 1)

    if facts_row:
        lane_at = lax.broadcasted_iota(jnp.int32, (1, LANES), 1)
        facts = jnp.zeros((1, LANES), jnp.float32)
        for t in range(tiles):
            facts = jnp.where(lane_at == t, event_ref[t].astype(jnp.float32), facts)
            facts = jnp.where(lane_at == tiles + t, live_ref[t].astype(jnp.float32), facts)
        for d in range(cols // HALF):
            out_ref[d * stride + tiles : d * stride + tiles + 1, :] = facts


def tile_stats(summary, kernel, grid_offset, log_prior, tile_event, tile_live, part):
    rows, depth = summary.shape
    cols = kernel.shape[1] // 2
    facts_row = 1 - part
    tiles = tile_event.shape[0]
    tile_rows = rows // tiles
    stride = tiles + facts_row
    hbm = pl.BlockSpec(memory_space=pltpu.HBM)
    f32 = jnp.float32
    lanes = BLOCK // LANES
    groups = (rows + CHUNK) // GROUP
    return pl.pallas_call(
        functools.partial(stats_kernel, tiles, tile_rows, cols, part * cols, facts_row),
        out_shape=jax.ShapeDtypeStruct((cols // HALF * stride, LANES), f32),
        in_specs=[hbm] * 6,
        out_specs=pl.BlockSpec(memory_space=pltpu.VMEM),
        scratch_shapes=[
            pltpu.VMEM((rows + CHUNK, depth), jnp.bfloat16),
            pltpu.VMEM((cols // BLOCK, depth, BLOCK), jnp.bfloat16),
            pltpu.VMEM((rows + CHUNK, LANES), f32),
            pltpu.VMEM((rows + CHUNK, BLOCK), f32),
            pltpu.VMEM((rows + CHUNK, BLOCK), f32),
            pltpu.VMEM((lanes * (8 * tiles + 8), LANES), f32),
            pltpu.VMEM((lanes * (tiles + 8), LANES), f32),
            pltpu.VMEM((2 * lanes * (8 * tiles + 8), LANES), f32),
            pltpu.VMEM((1, 2 * cols), f32),
            pltpu.VMEM((tiles, tile_rows), f32),
            pltpu.SMEM((tiles,), jnp.int32),
            pltpu.SMEM((tiles,), jnp.int32),
            pltpu.SMEM((groups,), jnp.int32),
            pltpu.SMEM((groups,), f32),
            pltpu.SMEM((tiles,), jnp.int32),
            pltpu.SemaphoreType.DMA((tiles, (tile_rows // GROUP).bit_length())),
            pltpu.SemaphoreType.DMA((cols // BLOCK,)),
            pltpu.SemaphoreType.DMA((4,)),
        ],
        cost_estimate=pl.CostEstimate(flops=rows * depth * cols, bytes_accessed=4 * rows * depth, transcendentals=0),
        compiler_params=pltpu.CompilerParams(vmem_limit_bytes=60 << 20),
    )(
        tile_event, tile_live, grid_offset.reshape(1, 2 * cols), log_prior.reshape(tiles, tile_rows), summary, kernel,
    )


def split3(x):
    high = x.astype(jnp.bfloat16)
    rest = x - high.astype(jnp.float32)
    middle = rest.astype(jnp.bfloat16)
    low = (rest - middle.astype(jnp.float32)).astype(jnp.bfloat16)
    return high, middle, low


def swap(x):
    return pltpu.roll(x, HALF, 1)


def join_events(level, event, chosen, ratio, peak):
    total = level.shape[0]
    peak[...] = jnp.zeros(peak.shape, jnp.float32)

    def find(step, carry):
        names = [(step * 4 + k).astype(jnp.float32) for k in range(4)]
        parts = [[jnp.full((8, LANES), NEG, jnp.float32) for _ in range(2)] for _ in range(4)]
        for v in range(total // 8):
            at = slice(v * 8, v * 8 + 8)
            whose, value = event[at, :], level[at, :]
            for k in range(4):
                parts[k][v % 2] = jnp.maximum(
                    parts[k][v % 2], jnp.where(whose == names[k], value, jnp.float32(NEG))
                )
        for k in range(4):
            best = jnp.max(jnp.maximum(parts[k][0], parts[k][1]), axis=0, keepdims=True)
            peak[pl.ds(step * 4 + k, 1), :] = jnp.maximum(best, swap(best))
        return carry

    lax.fori_loop(0, EVENTS // 4, find, 0)
    left = lax.broadcasted_iota(jnp.int32, (total, LANES), 1) < HALF
    found = jnp.dot(chosen, jnp.concatenate(split3(peak[...]), axis=1), preferred_element_type=jnp.float32)
    found = (found[:, :LANES] + found[:, LANES : 2 * LANES]) + found[:, 2 * LANES :]
    one = jnp.exp(level[...] - jnp.where(left, found[:total], found[total:]))
    two = ratio * one * one
    pieces = []
    for side in (left, ~left):
        pieces.append(jnp.concatenate(
            split3(jnp.where(side, one, jnp.float32(0))) + split3(jnp.where(side, two, jnp.float32(0))), axis=1
        ))
    right = jnp.concatenate(pieces, axis=0)
    sums = lax.dot_general(chosen, right, (((0,), (0,)), ((), ())), preferred_element_type=jnp.float32)
    part = [sums[:EVENTS, k * LANES : (k + 1) * LANES] for k in range(6)]
    first = (part[0] + part[1]) + part[2]
    second = (part[3] + part[4]) + part[5]
    return peak[:EVENTS, :], first + swap(first), second + swap(second)


def choose(low, high):
    names = lax.broadcasted_iota(jnp.int32, low.shape, 1).astype(jnp.float32)
    both = jnp.concatenate([low, high], axis=0)
    names = jnp.concatenate([names, names], axis=0)
    return jnp.where(both == names, jnp.float32(1), jnp.float32(0)).astype(jnp.bfloat16)


def merge_first_kernel(devices, tiles, got_ref, done_ref, event_ref, level, event, peak):
    half = tiles // 2
    stride = tiles + 1
    total = devices * half
    facts = got_ref[pl.ds(tiles, devices, stride=stride), :]
    left = lax.broadcasted_iota(jnp.int32, (devices, LANES), 1) < HALF
    live = []
    for k in range(2):
        for i in range(half):
            t = k * half + i
            spread = jnp.broadcast_to(facts[:, t : t + 1], (devices, LANES))
            event_ref[(k * half + i) * devices : (k * half + i + 1) * devices, :] = spread
            live.append(jnp.broadcast_to(facts[:, tiles + t : tiles + t + 1], (devices, LANES)))
    for i in range(half):
        at = slice(i * devices, (i + 1) * devices)
        level[at, :] = got_ref[pl.ds(i, devices, stride=stride), :]
        event[at, :] = jnp.where(left, event_ref[at, :], event_ref[total + i * devices : total + (i + 1) * devices, :])
    ratio = jnp.concatenate([got_ref[pl.ds(half + i, devices, stride=stride), :] for i in range(half)], axis=0)
    chosen = choose(event_ref[:total, :], event_ref[total:, :])
    top, first, second = join_events(level, event, chosen, ratio, peak)
    live = jnp.concatenate(live, axis=0).astype(jnp.bfloat16)
    count = lax.dot_general(chosen, live, (((0,), (0,)), ((), ())), preferred_element_type=jnp.float32)[:EVENTS]
    done_ref[:EVENTS, :] = top + jnp.log(first) - jnp.log(count)
    done_ref[EVENTS : 2 * EVENTS, :] = first * first / (second * count)
    done_ref[2 * EVENTS :, :] = count


def merge_second_kernel(devices, tiles, got_ref, done_ref, event_ref, out_ref, level, event, peak, kept):
    half = tiles // 2
    total = devices * half
    left = lax.broadcasted_iota(jnp.int32, (devices, LANES), 1) < HALF
    for i in range(half):
        at = slice(i * devices, (i + 1) * devices)
        level[at, :] = got_ref[pl.ds(i, devices, stride=tiles), :]
        event[at, :] = jnp.where(left, event_ref[at, :], event_ref[total + i * devices : total + (i + 1) * devices, :])
    ratio = jnp.concatenate([got_ref[pl.ds(half + i, devices, stride=tiles), :] for i in range(half)], axis=0)
    chosen = choose(event_ref[:total, :], event_ref[total:, :])
    top, first, second = join_events(level, event, chosen, ratio, peak)
    count = done_ref[2 * EVENTS :, :]
    left = lax.broadcasted_iota(jnp.int32, (EVENTS, LANES), 1) < HALF
    evidence = jnp.where(left, done_ref[:EVENTS, :], top + jnp.log(first) - jnp.log(count))
    kept[:EVENTS, :] = evidence
    kept[EVENTS:, :] = jnp.where(left, done_ref[EVENTS : 2 * EVENTS, :], first * first / (second * count))
    own = EVENTS // devices
    out_stride = 2 * own + 1
    for k in range(own):
        out_ref[pl.ds(k, devices, stride=out_stride), :] = kept[pl.ds(k, devices, stride=own), :]
        out_ref[pl.ds(own + k, devices, stride=out_stride), :] = kept[pl.ds(EVENTS + k, devices, stride=own), :]
    loglik = jnp.sum(evidence, axis=0, keepdims=True) / jnp.float32(EVENTS)
    out_ref[pl.ds(2 * own, devices, stride=out_stride), :] = jnp.broadcast_to(loglik, (devices, LANES))


def merge_first(got, devices, tiles):
    f32 = jnp.float32
    vmem = pl.BlockSpec(memory_space=pltpu.VMEM)
    total = devices * tiles // 2
    return pl.pallas_call(
        functools.partial(merge_first_kernel, devices, tiles),
        out_shape=(
            jax.ShapeDtypeStruct((3 * EVENTS, LANES), f32),
            jax.ShapeDtypeStruct((2 * total, LANES), f32),
        ),
        in_specs=[vmem],
        out_specs=(vmem, vmem),
        scratch_shapes=[pltpu.VMEM((total, LANES), f32), pltpu.VMEM((total, LANES), f32), pltpu.VMEM((LANES, LANES), f32)],
        cost_estimate=pl.CostEstimate(flops=400_000_000, bytes_accessed=1_000_000, transcendentals=0),
        compiler_params=pltpu.CompilerParams(vmem_limit_bytes=8 << 20),
    )(got)


def merge_second(got, done, event, devices, tiles):
    f32 = jnp.float32
    vmem = pl.BlockSpec(memory_space=pltpu.VMEM)
    total = devices * tiles // 2
    return pl.pallas_call(
        functools.partial(merge_second_kernel, devices, tiles),
        out_shape=jax.ShapeDtypeStruct((devices * (2 * (EVENTS // devices) + 1), LANES), f32),
        in_specs=[vmem] * 3,
        out_specs=vmem,
        scratch_shapes=[
            pltpu.VMEM((total, LANES), f32),
            pltpu.VMEM((total, LANES), f32),
            pltpu.VMEM((LANES, LANES), f32),
            pltpu.VMEM((2 * EVENTS, LANES), f32),
        ],
        compiler_params=pltpu.CompilerParams(vmem_limit_bytes=8 << 20),
    )(got, done, event)


def last_kernel(devices, own, got_ref, evidence_ref, ess_ref, posterior_ref):
    stride = 2 * own + 1
    cols = devices * LANES
    left = lax.broadcasted_iota(jnp.int32, (own, LANES), 1) < HALF
    for g in range(devices // 2):
        for k, ref in enumerate((evidence_ref, ess_ref)):
            even = got_ref[2 * g * stride + k * own : 2 * g * stride + (k + 1) * own, :]
            odd = got_ref[(2 * g + 1) * stride + k * own : (2 * g + 1) * stride + (k + 1) * own, :]
            ref[:, g * LANES : (g + 1) * LANES] = jnp.where(left, even, swap(odd))
            ref[:, cols // 2 + g * LANES : cols // 2 + (g + 1) * LANES] = jnp.where(left, swap(even), odd)
    even = got_ref[pl.ds(2 * own, devices // 2, stride=2 * stride), :]
    odd = got_ref[pl.ds(2 * own + stride, devices // 2, stride=2 * stride), :]
    left = lax.broadcasted_iota(jnp.int32, (devices // 2, LANES), 1) < HALF
    loglik = jnp.concatenate([jnp.where(left, even, swap(odd)), jnp.where(left, swap(even), odd)], axis=0)
    top = jnp.max(jnp.max(loglik, axis=0, keepdims=True), axis=1, keepdims=True)
    mass = jnp.exp(loglik - top)
    mass = jnp.sum(jnp.sum(mass, axis=0, keepdims=True), axis=1, keepdims=True)
    posterior_ref[...] = loglik - (top + jnp.log(mass))


def last(got, devices, own):
    f32 = jnp.float32
    vmem = pl.BlockSpec(memory_space=pltpu.VMEM)
    cols = devices * LANES
    return pl.pallas_call(
        functools.partial(last_kernel, devices, own),
        out_shape=(
            jax.ShapeDtypeStruct((own, cols), f32),
            jax.ShapeDtypeStruct((own, cols), f32),
            jax.ShapeDtypeStruct((devices, LANES), f32),
        ),
        in_specs=[vmem],
        out_specs=(vmem, vmem, vmem),
        compiler_params=pltpu.CompilerParams(vmem_limit_bytes=8 << 20),
    )(got)


def exchange(x, devices):
    width = x.shape[0] // devices * LANES
    got = lax.all_to_all(x.reshape(devices, 1, width), "samp", split_axis=0, concat_axis=0, tiled=True)
    return got.reshape(x.shape)


def column_body(devices, *args):
    tiles = args[4].shape[0]
    sent = tile_stats(*args, 0)
    got = exchange(sent, devices)
    more = tile_stats(*args, 1)
    rest = exchange(more, devices)
    done, event = merge_first(got, devices, tiles)
    merged = merge_second(rest, done, event, devices, tiles)
    evidence, ess, posterior = last(exchange(merged, devices), devices, EVENTS // devices)
    return evidence, ess, posterior.reshape(-1)


def row_body(summary, kernel, grid_offset, log_prior, tile_event, tile_live):
    row_count = summary.shape[0]
    grid_cols = kernel.shape[1]
    tile_count = tile_event.shape[0]
    tile_rows = row_count // tile_count
    scores = jnp.dot(summary, kernel, preferred_element_type=jnp.float32)
    scores = scores + grid_offset[None, :] - log_prior[:, None]
    scores = scores.reshape(tile_count, tile_rows, grid_cols)
    is_live = lax.broadcasted_iota(jnp.int32, (tile_count, tile_rows), 1) < tile_live[:, None]
    masked = jnp.where(is_live[:, :, None], scores, jnp.float32(-1e30))
    tile_max = jnp.max(masked, axis=1)
    shifted = jnp.exp(masked - tile_max[:, None, :])
    tile_first = jnp.sum(shifted, axis=1)
    tile_second = jnp.sum(shifted * shifted, axis=1)
    member = tile_event[None, :] == lax.broadcasted_iota(jnp.int32, (EVENTS, tile_count), 0)
    local_peak = jnp.max(
        jnp.where(member[:, :, None], tile_max[None, :, :], jnp.float32(-1e30)), axis=1
    )
    live_count = jnp.sum(jnp.where(member, tile_live[None, :], 0), axis=1).astype(jnp.float32)
    factor = jnp.exp(tile_max - local_peak[tile_event])
    member_float = member.astype(jnp.float32)
    local_first = jnp.dot(member_float, tile_first * factor, precision=lax.Precision.HIGHEST)
    local_second = jnp.dot(
        member_float, tile_second * factor * factor, precision=lax.Precision.HIGHEST
    )
    got_peak, got_first, got_second, got_count = (
        lax.all_to_all(local_peak[:, None, :], "samp", split_axis=0, concat_axis=1, tiled=True),
        lax.all_to_all(local_first[:, None, :], "samp", split_axis=0, concat_axis=1, tiled=True),
        lax.all_to_all(local_second[:, None, :], "samp", split_axis=0, concat_axis=1, tiled=True),
        lax.all_to_all(live_count[:, None, None], "samp", split_axis=0, concat_axis=1, tiled=True),
    )
    event_peak = jnp.max(got_peak, axis=1)
    rescale = jnp.exp(got_peak - event_peak[:, None, :])
    first_sum = jnp.sum(got_first * rescale, axis=1)
    second_sum = jnp.sum(got_second * rescale * rescale, axis=1)
    total_live = jnp.sum(got_count[:, :, 0], axis=1)
    log_evidence = event_peak + jnp.log(first_sum) - jnp.log(total_live)[:, None]
    ess_fraction = first_sum * first_sum / (second_sum * total_live[:, None])
    loglik = lax.psum(jnp.sum(log_evidence, axis=0), "samp") / jnp.float32(EVENTS)
    local_top = jnp.max(loglik)
    grid_top = lax.pmax(local_top, "grid")
    grid_mass = lax.psum(jnp.sum(jnp.exp(loglik - grid_top)), "grid")
    log_posterior = loglik - (grid_top + jnp.log(grid_mass))
    return (log_evidence, ess_fraction, log_posterior)


def solution(mesh):
    in_specs = (P("samp", None), P(None, "grid"), P("grid"), P("samp"), P("samp"), P("samp"))
    out_specs = (P("samp", "grid"), P("samp", "grid"), P("grid"))
    devices = mesh.shape["samp"]

    def body(summary, kernel, *rest):
        tiles, cols = rest[2].shape[0], kernel.shape[1]
        fits = (
            mesh.shape["grid"] == 1
            and cols == devices * LANES
            and cols % (4 * BLOCK) == 0
            and summary.shape[0] == tiles * LANES
            and tiles % 16 == 0
            and EVENTS % devices == 0
        )
        if fits:
            return column_body(devices, summary, kernel, *rest)
        return row_body(summary, kernel, *rest)

    return jax.shard_map(body, mesh=mesh, in_specs=in_specs, out_specs=out_specs, check_vma=False)
```

```python
import functools

import jax
import jax.numpy as jnp
from jax import lax
from jax.experimental import pallas as pl
from jax.experimental.pallas import tpu as pltpu
from jax.sharding import PartitionSpec as P

EVENTS = 64
LANES = 128
GROUP = 16
CHUNK = 256
BLOCK = 1024
UNROLL = 2
NEG = -1e30
DEAD = 1e30


def stats_kernel(
    tiles, tile_rows, depth, cols, event_hbm, live_hbm, offset_hbm, prior_hbm, summary_ref, kernel_ref,
    out_ref, lhs, rhs, prior, score_a, score_b, top, peak, held_sums, offset_ref, prior_ref,
    event_ref, live_ref, owner, fresh, start, row_sem, col_sem, fact_sem,
):
    blocks = cols // BLOCK
    per_tile = tile_rows // GROUP
    sizes = [1 << k for k in reversed(range(per_tile.bit_length()))]
    stride = 2 * tiles + 1
    lanes = BLOCK // LANES
    span = 8 * tiles + 8
    peak_span = tiles + 8
    parts = lanes // 2
    chunk_groups = CHUNK // GROUP

    facts = [
        pltpu.make_async_copy(source, target, fact_sem.at[k])
        for k, (source, target) in enumerate(
            ((live_hbm, live_ref), (event_hbm, event_ref), (prior_hbm, prior_ref), (offset_hbm, offset_ref))
        )
    ]
    for copy in facts:
        copy.start()

    def col_copy(n):
        return pltpu.make_async_copy(kernel_ref.at[:, pl.ds(n * BLOCK, BLOCK)], rhs.at[n], col_sem.at[n])

    col_copy(0).start()

    def row_copies(act):
        for t in range(tiles):
            count = lax.div(live_ref[t] + (GROUP - 1), GROUP)
            base = start[t]
            for k, size in enumerate(sizes):
                done = lax.bitwise_and(count, ~(2 * size - 1))

                @pl.when(lax.bitwise_and(count, size) != 0)
                def _():
                    copy = pltpu.make_async_copy(
                        summary_ref.at[pl.ds(pl.multiple_of(t * tile_rows + done * GROUP, GROUP), size * GROUP)],
                        lhs.at[pl.ds(pl.multiple_of((base + done) * GROUP, GROUP), size * GROUP)],
                        row_sem.at[t, k],
                    )
                    act(copy)

    facts[0].wait()
    total = jnp.int32(0)
    for t in range(tiles):
        start[t] = total
        total = total + lax.div(live_ref[t] + (GROUP - 1), GROUP)
    row_copies(lambda copy: copy.start())
    for n in range(1, blocks):
        col_copy(n).start()
    for copy in facts[1:]:
        copy.wait()

    chunks = lax.div(total + (chunk_groups - 1), chunk_groups)
    for t in range(tiles):
        count = lax.div(live_ref[t] + (GROUP - 1), GROUP)

        def mark(j, carry):
            owner[start[t] + j] = t
            fresh[start[t] + j] = jnp.where(j == 0, jnp.float32(0), jnp.float32(1))
            return carry

        lax.fori_loop(0, count, mark, 0)
        row_at = lax.broadcasted_iota(jnp.int32, (1, tile_rows), 1)
        held = jnp.where(row_at < live_ref[t], prior_ref[t : t + 1, :], jnp.float32(DEAD))
        spread = jnp.broadcast_to(held, (LANES, tile_rows)).T
        prior[pl.ds(pl.multiple_of(start[t] * GROUP, GROUP), tile_rows), :] = spread
    for j in range(chunk_groups):
        owner[total + j] = tiles
        fresh[total + j] = jnp.float32(0)

    top[...] = jnp.zeros(top.shape, jnp.float32)
    held_sums[...] = jnp.zeros(held_sums.shape, jnp.float32)
    peak[...] = jnp.zeros(peak.shape, jnp.float32)
    row_copies(lambda copy: copy.wait())

    def rows_at(c, g):
        return pl.ds(pl.multiple_of(c * CHUNK, CHUNK) + g * GROUP, GROUP)

    def tops_open(c):
        base = pl.multiple_of(owner[c * chunk_groups] * 8, 8)
        return [top[pl.ds(base + lane * span, 8), :] for lane in range(lanes)]

    def products(n, c, count, score, h, held):
        rows = lhs[pl.ds(pl.multiple_of(c * CHUNK, CHUNK), count * CHUNK), :]
        part = jnp.dot(rows, rhs[n, :, h * 256 : (h + 1) * 256], preferred_element_type=jnp.float32)
        for g in range(count * chunk_groups):
            base = pl.multiple_of(owner[c * chunk_groups + g] * 8, 8)
            reset = fresh[c * chunk_groups + g] * jnp.float32(DEAD) - jnp.float32(DEAD)
            cost = prior[rows_at(c, g), :]
            for w in range(2):
                lane = h * 2 + w
                value = part[g * GROUP : (g + 1) * GROUP, w * LANES : (w + 1) * LANES] - cost
                score[rows_at(c, g), lane * LANES : (lane + 1) * LANES] = value
                held[lane] = jnp.maximum(held[lane] + reset, jnp.maximum(value[:8], value[8:]))
                top[pl.ds(base + lane * span, 8), :] = held[lane]

    def sums_open(c):
        base = pl.multiple_of(owner[c * chunk_groups] * 8, 8)
        return [
            [held_sums[pl.ds(base + (k * lanes + lane) * span, 8), :] for lane in range(lanes)] for k in range(2)
        ]

    def sums(c, count, score, part, held):
        one, two = held
        total_groups = count * chunk_groups
        for g in range(part * total_groups // parts, (part + 1) * total_groups // parts):
            tile = owner[c * chunk_groups + g]
            base = pl.multiple_of(tile * 8, 8)
            keep = fresh[c * chunk_groups + g]
            for lane in range(lanes):
                level = peak[pl.ds(tile + lane * peak_span, 8, stride=0), :]
                value = score[rows_at(c, g), lane * LANES : (lane + 1) * LANES]
                low, high = jnp.exp(value[:8] - level), jnp.exp(value[8:] - level)
                one[lane] = one[lane] * keep + (low + high)
                two[lane] = two[lane] * keep + (low * low + high * high)
                held_sums[pl.ds(base + lane * span, 8), :] = one[lane]
                held_sums[pl.ds(base + (lanes + lane) * span, 8), :] = two[lane]

    def fold(ref, half, w, join):
        kept = [ref[pl.ds(w * span + half * 64 + i, 8, stride=8), :] for i in range(8)]
        while len(kept) > 1:
            kept = [join(a, b) for a, b in zip(kept[::2], kept[1::2])]
        return kept[0]

    def close_top():
        for half in range(tiles // 8):
            for w in range(lanes):
                peak[pl.ds(w * peak_span + half * 8, 8), :] = fold(top, half, w, jnp.maximum)

    def close_sums(n):
        for half in range(tiles // 8):
            for w in range(lanes):
                one = fold(held_sums, half, w, jnp.add)
                two = fold(held_sums, half, lanes + w, jnp.add)
                level = peak[pl.ds(w * peak_span + half * 8, 8), :]
                shift = offset_ref[:, pl.ds(pl.multiple_of(n * BLOCK + w * LANES, LANES), LANES)]
                base = (n * lanes + w) * stride + half * 8
                out_ref[pl.ds(base, 8), :] = level + jnp.log(one) + shift
                out_ref[pl.ds(base + tiles, 8), :] = two / (one * one)

    def each_chunk(work):
        def step(i, carry):
            work(i * UNROLL, UNROLL)
            return carry

        bulk = lax.div(chunks, UNROLL)
        lax.fori_loop(0, bulk, step, 0)

        def tail(c, carry):
            work(c, 1)
            return carry

        lax.fori_loop(bulk * UNROLL, chunks, tail, 0)

    def only_products(c, count):
        held = tops_open(c)
        for h in range(parts):
            products(0, c, count, score_a, h, held)

    def only_sums(c, count):
        held = sums_open(c)
        for h in range(parts):
            sums(c, count, score_b, h, held)

    col_copy(0).wait()
    each_chunk(only_products)

    def step(n, now, before):
        close_top()
        col_copy(n).wait()

        def work(c, count):
            held = sums_open(c)
            tops = tops_open(c)
            for h in range(parts):
                sums(c, count, before, h, held)
                products(n, c, count, now, h, tops)

        each_chunk(work)
        close_sums(n - 1)

    def pair(i, carry):
        step(2 * i + 1, score_b, score_a)

        @pl.when(i < blocks // 2 - 1)
        def _():
            step(2 * i + 2, score_a, score_b)

        return carry

    lax.fori_loop(0, blocks // 2, pair, 0)
    close_top()
    each_chunk(only_sums)
    close_sums(blocks - 1)

    lane_at = lax.broadcasted_iota(jnp.int32, (1, LANES), 1)
    facts = jnp.zeros((1, LANES), jnp.float32)
    for t in range(tiles):
        facts = jnp.where(lane_at == t, event_ref[t].astype(jnp.float32), facts)
        facts = jnp.where(lane_at == tiles + t, live_ref[t].astype(jnp.float32), facts)
    for d in range(cols // LANES):
        out_ref[d * stride + 2 * tiles : d * stride + 2 * tiles + 1, :] = facts


def tile_stats(summary, kernel, grid_offset, log_prior, tile_event, tile_live):
    rows, depth = summary.shape
    cols = kernel.shape[1]
    tiles = tile_event.shape[0]
    tile_rows = rows // tiles
    stride = 2 * tiles + 1
    hbm = pl.BlockSpec(memory_space=pltpu.HBM)
    f32 = jnp.float32
    lanes = BLOCK // LANES
    groups = (rows + CHUNK) // GROUP
    return pl.pallas_call(
        functools.partial(stats_kernel, tiles, tile_rows, depth, cols),
        out_shape=jax.ShapeDtypeStruct((cols // LANES * stride, LANES), f32),
        in_specs=[hbm] * 6,
        out_specs=pl.BlockSpec(memory_space=pltpu.VMEM),
        scratch_shapes=[
            pltpu.VMEM((rows + CHUNK, depth), jnp.bfloat16),
            pltpu.VMEM((cols // BLOCK, depth, BLOCK), jnp.bfloat16),
            pltpu.VMEM((rows + CHUNK, LANES), f32),
            pltpu.VMEM((rows + CHUNK, BLOCK), f32),
            pltpu.VMEM((rows + CHUNK, BLOCK), f32),
            pltpu.VMEM((lanes * (8 * tiles + 8), LANES), f32),
            pltpu.VMEM((lanes * (tiles + 8), LANES), f32),
            pltpu.VMEM((2 * lanes * (8 * tiles + 8), LANES), f32),
            pltpu.VMEM((1, cols), f32),
            pltpu.VMEM((tiles, tile_rows), f32),
            pltpu.SMEM((tiles,), jnp.int32),
            pltpu.SMEM((tiles,), jnp.int32),
            pltpu.SMEM((groups,), jnp.int32),
            pltpu.SMEM((groups,), f32),
            pltpu.SMEM((tiles,), jnp.int32),
            pltpu.SemaphoreType.DMA((tiles, (tile_rows // GROUP).bit_length())),
            pltpu.SemaphoreType.DMA((cols // BLOCK,)),
            pltpu.SemaphoreType.DMA((4,)),
        ],
        compiler_params=pltpu.CompilerParams(vmem_limit_bytes=60 << 20),
    )(
        tile_event, tile_live, grid_offset.reshape(1, cols), log_prior.reshape(tiles, tile_rows), summary, kernel,
    )


def split3(x):
    high = x.astype(jnp.bfloat16)
    rest = x - high.astype(jnp.float32)
    middle = rest.astype(jnp.bfloat16)
    low = (rest - middle.astype(jnp.float32)).astype(jnp.bfloat16)
    return high, middle, low


def merge_kernel(devices, tiles, got_ref, out_ref, level, event, peak, kept):
    stride = 2 * tiles + 1
    total = devices * tiles
    facts = got_ref[pl.ds(2 * tiles, devices, stride=stride), :]
    for i in range(tiles):
        at = slice(i * devices, (i + 1) * devices)
        level[at, :] = got_ref[pl.ds(i, devices, stride=stride), :]
        event[at, :] = jnp.broadcast_to(facts[:, i : i + 1], (devices, LANES))
    peak[...] = jnp.zeros(peak.shape, jnp.float32)

    def find(step, carry):
        names = [(step * 2 + k).astype(jnp.float32) for k in range(2)]
        parts = [[jnp.full((8, LANES), NEG, jnp.float32) for _ in range(2)] for _ in range(2)]
        for v in range(total // 8):
            at = slice(v * 8, v * 8 + 8)
            whose, value = event[at, :], level[at, :]
            for k in range(2):
                parts[k][v % 2] = jnp.maximum(
                    parts[k][v % 2], jnp.where(whose == names[k], value, jnp.float32(NEG))
                )
        for k in range(2):
            best = jnp.max(jnp.maximum(parts[k][0], parts[k][1]), axis=0, keepdims=True)
            peak[pl.ds(step * 2 + k, 1), :] = best
        return carry

    lax.fori_loop(0, EVENTS // 2, find, 0)
    names = lax.broadcasted_iota(jnp.int32, (total, LANES), 1).astype(jnp.float32)
    chosen = jnp.where(event[...] == names, jnp.float32(1), jnp.float32(0)).astype(jnp.bfloat16)
    found = jnp.dot(chosen, jnp.concatenate(split3(peak[...]), axis=1), preferred_element_type=jnp.float32)
    shift = (found[:, :LANES] + found[:, LANES : 2 * LANES]) + found[:, 2 * LANES :]
    one = jnp.exp(level[...] - shift)
    ratio = [got_ref[pl.ds(tiles + i, devices, stride=stride), :] for i in range(tiles)]
    two = jnp.concatenate(ratio, axis=0) * one * one
    live = [jnp.broadcast_to(facts[:, tiles + i : tiles + i + 1], (devices, LANES)) for i in range(tiles)]
    live = jnp.concatenate(live, axis=0).astype(jnp.bfloat16)
    right = jnp.concatenate(split3(one) + split3(two) + (live,), axis=1)
    sums = lax.dot_general(chosen, right, (((0,), (0,)), ((), ())), preferred_element_type=jnp.float32)
    part = [sums[:EVENTS, k * LANES : (k + 1) * LANES] for k in range(7)]
    first = part[0] + part[1] + part[2]
    second = part[3] + part[4] + part[5]
    count = part[6]
    evidence = peak[:EVENTS, :] + jnp.log(first) - jnp.log(count)
    kept[:EVENTS, :] = evidence
    kept[EVENTS:, :] = first * first / (second * count)
    own = EVENTS // devices
    out_stride = 2 * own + 1
    for k in range(own):
        out_ref[pl.ds(k, devices, stride=out_stride), :] = kept[pl.ds(k, devices, stride=own), :]
        out_ref[pl.ds(own + k, devices, stride=out_stride), :] = kept[pl.ds(EVENTS + k, devices, stride=own), :]
    loglik = jnp.sum(evidence, axis=0, keepdims=True) / jnp.float32(EVENTS)
    out_ref[pl.ds(2 * own, devices, stride=out_stride), :] = jnp.broadcast_to(loglik, (devices, LANES))


def merge(got, devices, tiles):
    total = devices * tiles
    f32 = jnp.float32
    vmem = pl.BlockSpec(memory_space=pltpu.VMEM)
    return pl.pallas_call(
        functools.partial(merge_kernel, devices, tiles),
        out_shape=jax.ShapeDtypeStruct((devices * (2 * (EVENTS // devices) + 1), LANES), f32),
        in_specs=[vmem],
        out_specs=vmem,
        scratch_shapes=[
            pltpu.VMEM((total, LANES), f32),
            pltpu.VMEM((total, LANES), f32),
            pltpu.VMEM((LANES, LANES), f32),
            pltpu.VMEM((2 * EVENTS, LANES), f32),
        ],
        compiler_params=pltpu.CompilerParams(vmem_limit_bytes=8 << 20),
    )(got)


def last_kernel(devices, own, got_ref, evidence_ref, ess_ref, posterior_ref):
    stride = 2 * own + 1
    for d in range(devices):
        lane = slice(d * LANES, (d + 1) * LANES)
        evidence_ref[:, lane] = got_ref[d * stride : d * stride + own, :]
        ess_ref[:, lane] = got_ref[d * stride + own : d * stride + 2 * own, :]
    loglik = got_ref[pl.ds(2 * own, devices, stride=stride), :]
    top = jnp.max(jnp.max(loglik, axis=0, keepdims=True), axis=1, keepdims=True)
    mass = jnp.exp(loglik - top)
    mass = jnp.sum(jnp.sum(mass, axis=0, keepdims=True), axis=1, keepdims=True)
    posterior_ref[...] = loglik - (top + jnp.log(mass))


def last(got, devices, own):
    f32 = jnp.float32
    vmem = pl.BlockSpec(memory_space=pltpu.VMEM)
    cols = devices * LANES
    return pl.pallas_call(
        functools.partial(last_kernel, devices, own),
        out_shape=(
            jax.ShapeDtypeStruct((own, cols), f32),
            jax.ShapeDtypeStruct((own, cols), f32),
            jax.ShapeDtypeStruct((devices, LANES), f32),
        ),
        in_specs=[vmem],
        out_specs=(vmem, vmem, vmem),
        compiler_params=pltpu.CompilerParams(vmem_limit_bytes=8 << 20),
    )(got)


def exchange(x, devices):
    width = x.shape[0] // devices * LANES
    got = lax.all_to_all(x.reshape(devices, 1, width), "samp", split_axis=0, concat_axis=0, tiled=True)
    return got.reshape(x.shape)


def column_body(devices, summary, kernel, grid_offset, log_prior, tile_event, tile_live):
    tiles = tile_event.shape[0]
    own = EVENTS // devices
    sent = tile_stats(summary, kernel, grid_offset, log_prior, tile_event, tile_live)
    merged = merge(exchange(sent, devices), devices, tiles)
    evidence, ess, posterior = last(exchange(merged, devices), devices, own)
    return evidence, ess, posterior.reshape(-1)


def row_body(summary, kernel, grid_offset, log_prior, tile_event, tile_live):
    row_count = summary.shape[0]
    grid_cols = kernel.shape[1]
    tile_count = tile_event.shape[0]
    tile_rows = row_count // tile_count
    scores = jnp.dot(summary, kernel, preferred_element_type=jnp.float32)
    scores = scores + grid_offset[None, :] - log_prior[:, None]
    scores = scores.reshape(tile_count, tile_rows, grid_cols)
    is_live = lax.broadcasted_iota(jnp.int32, (tile_count, tile_rows), 1) < tile_live[:, None]
    masked = jnp.where(is_live[:, :, None], scores, jnp.float32(-1e30))
    tile_max = jnp.max(masked, axis=1)
    shifted = jnp.exp(masked - tile_max[:, None, :])
    tile_first = jnp.sum(shifted, axis=1)
    tile_second = jnp.sum(shifted * shifted, axis=1)
    member = tile_event[None, :] == lax.broadcasted_iota(jnp.int32, (EVENTS, tile_count), 0)
    local_peak = jnp.max(
        jnp.where(member[:, :, None], tile_max[None, :, :], jnp.float32(-1e30)), axis=1
    )
    live_count = jnp.sum(jnp.where(member, tile_live[None, :], 0), axis=1).astype(jnp.float32)
    factor = jnp.exp(tile_max - local_peak[tile_event])
    member_float = member.astype(jnp.float32)
    local_first = jnp.dot(member_float, tile_first * factor, precision=lax.Precision.HIGHEST)
    local_second = jnp.dot(
        member_float, tile_second * factor * factor, precision=lax.Precision.HIGHEST
    )
    got_peak, got_first, got_second, got_count = (
        lax.all_to_all(local_peak[:, None, :], "samp", split_axis=0, concat_axis=1, tiled=True),
        lax.all_to_all(local_first[:, None, :], "samp", split_axis=0, concat_axis=1, tiled=True),
        lax.all_to_all(local_second[:, None, :], "samp", split_axis=0, concat_axis=1, tiled=True),
        lax.all_to_all(live_count[:, None, None], "samp", split_axis=0, concat_axis=1, tiled=True),
    )
    event_peak = jnp.max(got_peak, axis=1)
    rescale = jnp.exp(got_peak - event_peak[:, None, :])
    first_sum = jnp.sum(got_first * rescale, axis=1)
    second_sum = jnp.sum(got_second * rescale * rescale, axis=1)
    total_live = jnp.sum(got_count[:, :, 0], axis=1)
    log_evidence = event_peak + jnp.log(first_sum) - jnp.log(total_live)[:, None]
    ess_fraction = first_sum * first_sum / (second_sum * total_live[:, None])
    loglik = lax.psum(jnp.sum(log_evidence, axis=0), "samp") / jnp.float32(EVENTS)
    local_top = jnp.max(loglik)
    grid_top = lax.pmax(local_top, "grid")
    grid_mass = lax.psum(jnp.sum(jnp.exp(loglik - grid_top)), "grid")
    log_posterior = loglik - (grid_top + jnp.log(grid_mass))
    return (log_evidence, ess_fraction, log_posterior)


def solution(mesh):
    in_specs = (P("samp", None), P(None, "grid"), P("grid"), P("samp"), P("samp"), P("samp"))
    out_specs = (P("samp", "grid"), P("samp", "grid"), P("grid"))
    devices = mesh.shape["samp"]

    def body(summary, kernel, *rest):
        tiles, cols = rest[2].shape[0], kernel.shape[1]
        fits = (
            mesh.shape["grid"] == 1
            and cols == devices * LANES
            and cols % (2 * BLOCK) == 0
            and summary.shape[0] == tiles * LANES
            and tiles % 8 == 0
            and EVENTS % devices == 0
        )
        if fits:
            return column_body(devices, summary, kernel, *rest)
        return row_body(summary, kernel, *rest)

    return jax.shard_map(body, mesh=mesh, in_specs=in_specs, out_specs=out_specs, check_vma=False)
```

```python
import functools

import jax
import jax.numpy as jnp
from jax import lax
from jax.experimental import pallas as pl
from jax.experimental.pallas import tpu as pltpu
from jax.sharding import PartitionSpec as P

EVENTS = 64
LANES = 128
GROUP = 16
CHUNK = 128
BLOCK = 1024
UNROLL = 4
NEG = -1e30
DEAD = 1e30


def stats_kernel(
    tiles, tile_rows, depth, cols, event_hbm, live_hbm, offset_hbm, prior_hbm, summary_ref, kernel_ref,
    out_hbm, built, raw, lhs, rhs, prior, score_a, score_b, top, peak, held_sums, offset_ref, prior_ref,
    event_ref, live_ref, owner, fresh, start, row_sem, col_sem, fact_sem, out_sem,
):
    blocks = cols // BLOCK
    per_tile = tile_rows // GROUP
    sizes = [1 << k for k in reversed(range(per_tile.bit_length()))]
    stride = 2 * tiles + 1
    lanes = BLOCK // LANES
    span = 8 * tiles + 8
    peak_span = tiles + 8
    parts = lanes // 2
    chunk_groups = CHUNK // GROUP

    facts = [
        pltpu.make_async_copy(source, target, fact_sem.at[k])
        for k, (source, target) in enumerate(
            ((live_hbm, live_ref), (event_hbm, event_ref), (prior_hbm, prior_ref), (offset_hbm, offset_ref))
        )
    ]
    for copy in facts:
        copy.start()

    def col_copy(n):
        return pltpu.make_async_copy(kernel_ref.at[:, pl.ds(n * BLOCK, BLOCK)], rhs.at[n], col_sem.at[n])

    col_copy(0).start()

    def row_copies(act):
        for t in range(tiles):
            count = lax.div(live_ref[t] + (GROUP - 1), GROUP)
            base = start[t]
            for k, size in enumerate(sizes):
                done = lax.bitwise_and(count, ~(2 * size - 1))

                @pl.when(lax.bitwise_and(count, size) != 0)
                def _():
                    copy = pltpu.make_async_copy(
                        summary_ref.at[pl.ds(pl.multiple_of(t * tile_rows + done * GROUP, GROUP), size * GROUP)],
                        raw.at[pl.ds(pl.multiple_of((base + done) * GROUP, GROUP), size * GROUP)],
                        row_sem.at[t, k],
                    )
                    act(copy)

    facts[0].wait()
    total = jnp.int32(0)
    for t in range(tiles):
        start[t] = total
        total = total + lax.div(live_ref[t] + (GROUP - 1), GROUP)
    row_copies(lambda copy: copy.start())
    for n in range(1, blocks):
        col_copy(n).start()
    for copy in facts[1:]:
        copy.wait()

    chunks = lax.div(total + (chunk_groups - 1), chunk_groups)
    for t in range(tiles):
        count = lax.div(live_ref[t] + (GROUP - 1), GROUP)

        def mark(j, carry):
            owner[start[t] + j] = t
            fresh[start[t] + j] = jnp.where(j == 0, jnp.float32(0), jnp.float32(1))
            return carry

        lax.fori_loop(0, count, mark, 0)
        row_at = lax.broadcasted_iota(jnp.int32, (1, tile_rows), 1)
        held = jnp.where(row_at < live_ref[t], prior_ref[t : t + 1, :], jnp.float32(DEAD))
        spread = jnp.broadcast_to(held, (LANES, tile_rows)).T
        prior[pl.ds(pl.multiple_of(start[t] * GROUP, GROUP), tile_rows), :] = spread
    for j in range(chunk_groups):
        owner[total + j] = tiles
        fresh[total + j] = jnp.float32(0)

    lane_at = lax.broadcasted_iota(jnp.int32, (1, LANES), 1)
    known = jnp.zeros((1, LANES), jnp.float32)
    for t in range(tiles):
        known = jnp.where(lane_at == t, event_ref[t].astype(jnp.float32), known)
        known = jnp.where(lane_at == tiles + t, live_ref[t].astype(jnp.float32), known)
    for d in range(cols // LANES):
        built[d * stride + 2 * tiles : d * stride + 2 * tiles + 1, :] = known

    top[...] = jnp.zeros(top.shape, jnp.float32)
    held_sums[...] = jnp.zeros(held_sums.shape, jnp.float32)
    peak[...] = jnp.zeros(peak.shape, jnp.float32)
    row_copies(lambda copy: copy.wait())

    def rows_at(c, g):
        return pl.ds(pl.multiple_of(c * CHUNK, CHUNK) + g * GROUP, GROUP)

    def tops_open(c):
        base = pl.multiple_of(owner[c * chunk_groups] * 8, 8)
        return [top[pl.ds(base + lane * span, 8), :] for lane in range(lanes)]

    def products(n, c, count, score, h, held):
        at = pl.ds(pl.multiple_of(c * CHUNK, CHUNK), count * CHUNK)
        rows = jnp.concatenate([lhs[k, at, :] for k in range(depth // LANES)], axis=1)
        part = jnp.dot(rows, rhs[n, :, h * 256 : (h + 1) * 256], preferred_element_type=jnp.float32)
        for g in range(count * chunk_groups):
            base = pl.multiple_of(owner[c * chunk_groups + g] * 8, 8)
            reset = fresh[c * chunk_groups + g] * jnp.float32(DEAD) - jnp.float32(DEAD)
            cost = prior[rows_at(c, g), :]
            for w in range(2):
                lane = h * 2 + w
                value = part[g * GROUP : (g + 1) * GROUP, w * LANES : (w + 1) * LANES] - cost
                score[rows_at(c, g), lane * LANES : (lane + 1) * LANES] = value
                held[lane] = jnp.maximum(held[lane] + reset, jnp.maximum(value[:8], value[8:]))
                top[pl.ds(base + lane * span, 8), :] = held[lane]

    def sums_open(c):
        base = pl.multiple_of(owner[c * chunk_groups] * 8, 8)
        return [
            [held_sums[pl.ds(base + (k * lanes + lane) * span, 8), :] for lane in range(lanes)] for k in range(2)
        ]

    def sums(c, count, score, part, held):
        one, two = held
        total_groups = count * chunk_groups
        for g in range(part * total_groups // parts, (part + 1) * total_groups // parts):
            tile = owner[c * chunk_groups + g]
            base = pl.multiple_of(tile * 8, 8)
            keep = fresh[c * chunk_groups + g]
            for lane in range(lanes):
                level = peak[pl.ds(tile + lane * peak_span, 8, stride=0), :]
                value = score[rows_at(c, g), lane * LANES : (lane + 1) * LANES]
                low, high = jnp.exp(value[:8] - level), jnp.exp(value[8:] - level)
                one[lane] = one[lane] * keep + (low + high)
                two[lane] = two[lane] * keep + (low * low + high * high)
                held_sums[pl.ds(base + lane * span, 8), :] = one[lane]
                held_sums[pl.ds(base + (lanes + lane) * span, 8), :] = two[lane]

    def fold(ref, half, w, join):
        kept = [ref[pl.ds(w * span + half * 64 + i, 8, stride=8), :] for i in range(8)]
        while len(kept) > 1:
            kept = [join(a, b) for a, b in zip(kept[::2], kept[1::2])]
        return kept[0]

    def close_top():
        for half in range(tiles // 8):
            for w in range(lanes):
                peak[pl.ds(w * peak_span + half * 8, 8), :] = fold(top, half, w, jnp.maximum)

    def close_sums(n):
        for half in range(tiles // 8):
            for w in range(lanes):
                one = fold(held_sums, half, w, jnp.add)
                two = fold(held_sums, half, lanes + w, jnp.add)
                level = peak[pl.ds(w * peak_span + half * 8, 8), :]
                shift = offset_ref[:, pl.ds(pl.multiple_of(n * BLOCK + w * LANES, LANES), LANES)]
                base = (n * lanes + w) * stride + half * 8
                built[pl.ds(base, 8), :] = level + jnp.log(one) + shift
                built[pl.ds(base + tiles, 8), :] = two / (one * one)

    def out_copy(n):
        size = lanes * stride
        at = pl.ds(pl.multiple_of(n * size, 8), size)
        return pltpu.make_async_copy(built.at[at], out_hbm.at[at], out_sem.at[n])

    def each_chunk(work):
        def step(i, carry):
            work(i * UNROLL, UNROLL)
            return carry

        lax.fori_loop(0, lax.div(chunks, UNROLL), step, 0)
        count = UNROLL // 2
        while count:
            first = lax.bitwise_and(chunks, ~(2 * count - 1))

            @pl.when(lax.bitwise_and(chunks, count) != 0)
            def _(first=first, count=count):
                work(first, count)

            count //= 2

    def only_products(c, count):
        held = tops_open(c)
        for g in range(count * chunk_groups):
            at = rows_at(c, g)
            for k in range(depth // LANES):
                lhs[k, at, :] = raw[at, k * LANES : (k + 1) * LANES]
        for h in range(parts):
            products(0, c, count, score_a, h, held)

    def only_sums(c, count):
        held = sums_open(c)
        for h in range(parts):
            sums(c, count, score_b, h, held)

    col_copy(0).wait()
    each_chunk(only_products)

    def step(n, now, before):
        close_top()
        col_copy(n).wait()

        def work(c, count):
            held = sums_open(c)
            tops = tops_open(c)
            for h in range(parts):
                sums(c, count, before, h, held)
                products(n, c, count, now, h, tops)

        each_chunk(work)
        close_sums(n - 1)
        out_copy(n - 1).start()

    def pair(i, carry):
        step(2 * i + 1, score_b, score_a)

        @pl.when(i < blocks // 2 - 1)
        def _():
            step(2 * i + 2, score_a, score_b)

        return carry

    lax.fori_loop(0, blocks // 2, pair, 0)
    close_top()
    each_chunk(only_sums)
    close_sums(blocks - 1)
    out_copy(blocks - 1).start()
    for n in range(blocks):
        out_copy(n).wait()


def tile_stats(summary, kernel, grid_offset, log_prior, tile_event, tile_live):
    rows, depth = summary.shape
    cols = kernel.shape[1]
    tiles = tile_event.shape[0]
    tile_rows = rows // tiles
    stride = 2 * tiles + 1
    hbm = pl.BlockSpec(memory_space=pltpu.HBM)
    f32 = jnp.float32
    lanes = BLOCK // LANES
    groups = (rows + CHUNK) // GROUP
    return pl.pallas_call(
        functools.partial(stats_kernel, tiles, tile_rows, depth, cols),
        out_shape=jax.ShapeDtypeStruct((cols // LANES * stride, LANES), f32),
        in_specs=[hbm] * 6,
        out_specs=hbm,
        scratch_shapes=[
            pltpu.VMEM((cols // LANES * stride, LANES), f32),
            pltpu.VMEM((rows + CHUNK, depth), jnp.bfloat16),
            pltpu.VMEM((depth // LANES, rows + CHUNK, LANES), jnp.bfloat16),
            pltpu.VMEM((cols // BLOCK, depth, BLOCK), jnp.bfloat16),
            pltpu.VMEM((rows + CHUNK, LANES), f32),
            pltpu.VMEM((rows + CHUNK, BLOCK), f32),
            pltpu.VMEM((rows + CHUNK, BLOCK), f32),
            pltpu.VMEM((lanes * (8 * tiles + 8), LANES), f32),
            pltpu.VMEM((lanes * (tiles + 8), LANES), f32),
            pltpu.VMEM((2 * lanes * (8 * tiles + 8), LANES), f32),
            pltpu.VMEM((1, cols), f32),
            pltpu.VMEM((tiles, tile_rows), f32),
            pltpu.SMEM((tiles,), jnp.int32),
            pltpu.SMEM((tiles,), jnp.int32),
            pltpu.SMEM((groups,), jnp.int32),
            pltpu.SMEM((groups,), f32),
            pltpu.SMEM((tiles,), jnp.int32),
            pltpu.SemaphoreType.DMA((tiles, (tile_rows // GROUP).bit_length())),
            pltpu.SemaphoreType.DMA((cols // BLOCK,)),
            pltpu.SemaphoreType.DMA((4,)),
            pltpu.SemaphoreType.DMA((cols // BLOCK,)),
        ],
        compiler_params=pltpu.CompilerParams(vmem_limit_bytes=60 << 20),
    )(
        tile_event, tile_live, grid_offset.reshape(1, cols), log_prior.reshape(tiles, tile_rows), summary, kernel,
    )


def split3(x):
    high = x.astype(jnp.bfloat16)
    rest = x - high.astype(jnp.float32)
    middle = rest.astype(jnp.bfloat16)
    low = (rest - middle.astype(jnp.float32)).astype(jnp.bfloat16)
    return high, middle, low


def merge_kernel(devices, tiles, got_ref, out_ref, level, event, peak, kept):
    stride = 2 * tiles + 1
    total = devices * tiles
    facts = got_ref[pl.ds(2 * tiles, devices, stride=stride), :]
    for i in range(tiles):
        at = slice(i * devices, (i + 1) * devices)
        level[at, :] = got_ref[pl.ds(i, devices, stride=stride), :]
        event[at, :] = jnp.broadcast_to(facts[:, i : i + 1], (devices, LANES))
    peak[...] = jnp.zeros(peak.shape, jnp.float32)

    def find(step, carry):
        names = [(step * 4 + k).astype(jnp.float32) for k in range(4)]
        parts = [[jnp.full((8, LANES), NEG, jnp.float32) for _ in range(2)] for _ in range(4)]
        for v in range(total // 8):
            at = slice(v * 8, v * 8 + 8)
            whose, value = event[at, :], level[at, :]
            for k in range(4):
                parts[k][v % 2] = jnp.maximum(
                    parts[k][v % 2], jnp.where(whose == names[k], value, jnp.float32(NEG))
                )
        for k in range(4):
            best = jnp.max(jnp.maximum(parts[k][0], parts[k][1]), axis=0, keepdims=True)
            peak[pl.ds(step * 4 + k, 1), :] = best
        return carry

    lax.fori_loop(0, EVENTS // 4, find, 0)
    names = lax.broadcasted_iota(jnp.int32, (total, LANES), 1).astype(jnp.float32)
    chosen = jnp.where(event[...] == names, jnp.float32(1), jnp.float32(0)).astype(jnp.bfloat16)
    found = jnp.dot(chosen, jnp.concatenate(split3(peak[...]), axis=1), preferred_element_type=jnp.float32)
    shift = (found[:, :LANES] + found[:, LANES : 2 * LANES]) + found[:, 2 * LANES :]
    one = jnp.exp(level[...] - shift)
    ratio = [got_ref[pl.ds(tiles + i, devices, stride=stride), :] for i in range(tiles)]
    two = jnp.concatenate(ratio, axis=0) * one * one
    live = [jnp.broadcast_to(facts[:, tiles + i : tiles + i + 1], (devices, LANES)) for i in range(tiles)]
    live = jnp.concatenate(live, axis=0).astype(jnp.bfloat16)
    right = jnp.concatenate(split3(one) + split3(two) + (live,), axis=1)
    sums = lax.dot_general(chosen, right, (((0,), (0,)), ((), ())), preferred_element_type=jnp.float32)
    part = [sums[:EVENTS, k * LANES : (k + 1) * LANES] for k in range(7)]
    first = part[0] + part[1] + part[2]
    second = part[3] + part[4] + part[5]
    count = part[6]
    evidence = peak[:EVENTS, :] + jnp.log(first) - jnp.log(count)
    kept[:EVENTS, :] = evidence
    kept[EVENTS:, :] = first * first / (second * count)
    own = EVENTS // devices
    out_stride = 2 * own + 1
    for k in range(own):
        out_ref[pl.ds(k, devices, stride=out_stride), :] = kept[pl.ds(k, devices, stride=own), :]
        out_ref[pl.ds(own + k, devices, stride=out_stride), :] = kept[pl.ds(EVENTS + k, devices, stride=own), :]
    loglik = jnp.sum(evidence, axis=0, keepdims=True) / jnp.float32(EVENTS)
    out_ref[pl.ds(2 * own, devices, stride=out_stride), :] = jnp.broadcast_to(loglik, (devices, LANES))


def merge(got, devices, tiles):
    total = devices * tiles
    f32 = jnp.float32
    vmem = pl.BlockSpec(memory_space=pltpu.VMEM)
    return pl.pallas_call(
        functools.partial(merge_kernel, devices, tiles),
        out_shape=jax.ShapeDtypeStruct((devices * (2 * (EVENTS // devices) + 1), LANES), f32),
        in_specs=[vmem],
        out_specs=vmem,
        scratch_shapes=[
            pltpu.VMEM((total, LANES), f32),
            pltpu.VMEM((total, LANES), f32),
            pltpu.VMEM((LANES, LANES), f32),
            pltpu.VMEM((2 * EVENTS, LANES), f32),
        ],
        compiler_params=pltpu.CompilerParams(vmem_limit_bytes=8 << 20),
    )(got)


def last_kernel(devices, own, got_ref, evidence_ref, ess_ref, posterior_ref):
    stride = 2 * own + 1
    for d in range(devices):
        lane = slice(d * LANES, (d + 1) * LANES)
        evidence_ref[:, lane] = got_ref[d * stride : d * stride + own, :]
        ess_ref[:, lane] = got_ref[d * stride + own : d * stride + 2 * own, :]
    loglik = got_ref[pl.ds(2 * own, devices, stride=stride), :]
    top = jnp.max(jnp.max(loglik, axis=0, keepdims=True), axis=1, keepdims=True)
    mass = jnp.exp(loglik - top)
    mass = jnp.sum(jnp.sum(mass, axis=0, keepdims=True), axis=1, keepdims=True)
    posterior_ref[...] = loglik - (top + jnp.log(mass))


def last(got, devices, own):
    f32 = jnp.float32
    vmem = pl.BlockSpec(memory_space=pltpu.VMEM)
    cols = devices * LANES
    return pl.pallas_call(
        functools.partial(last_kernel, devices, own),
        out_shape=(
            jax.ShapeDtypeStruct((own, cols), f32),
            jax.ShapeDtypeStruct((own, cols), f32),
            jax.ShapeDtypeStruct((devices, LANES), f32),
        ),
        in_specs=[vmem],
        out_specs=(vmem, vmem, vmem),
        compiler_params=pltpu.CompilerParams(vmem_limit_bytes=8 << 20),
    )(got)


def exchange(x, devices):
    width = x.shape[0] // devices * LANES
    got = lax.all_to_all(x.reshape(devices, 1, width), "samp", split_axis=0, concat_axis=0, tiled=True)
    return got.reshape(x.shape)


def column_body(devices, summary, kernel, grid_offset, log_prior, tile_event, tile_live):
    tiles = tile_event.shape[0]
    own = EVENTS // devices
    sent = tile_stats(summary, kernel, grid_offset, log_prior, tile_event, tile_live)
    merged = merge(exchange(sent, devices), devices, tiles)
    evidence, ess, posterior = last(exchange(merged, devices), devices, own)
    return evidence, ess, posterior.reshape(-1)


def row_body(summary, kernel, grid_offset, log_prior, tile_event, tile_live):
    row_count = summary.shape[0]
    grid_cols = kernel.shape[1]
    tile_count = tile_event.shape[0]
    tile_rows = row_count // tile_count
    scores = jnp.dot(summary, kernel, preferred_element_type=jnp.float32)
    scores = scores + grid_offset[None, :] - log_prior[:, None]
    scores = scores.reshape(tile_count, tile_rows, grid_cols)
    is_live = lax.broadcasted_iota(jnp.int32, (tile_count, tile_rows), 1) < tile_live[:, None]
    masked = jnp.where(is_live[:, :, None], scores, jnp.float32(-1e30))
    tile_max = jnp.max(masked, axis=1)
    shifted = jnp.exp(masked - tile_max[:, None, :])
    tile_first = jnp.sum(shifted, axis=1)
    tile_second = jnp.sum(shifted * shifted, axis=1)
    member = tile_event[None, :] == lax.broadcasted_iota(jnp.int32, (EVENTS, tile_count), 0)
    local_peak = jnp.max(
        jnp.where(member[:, :, None], tile_max[None, :, :], jnp.float32(-1e30)), axis=1
    )
    live_count = jnp.sum(jnp.where(member, tile_live[None, :], 0), axis=1).astype(jnp.float32)
    factor = jnp.exp(tile_max - local_peak[tile_event])
    member_float = member.astype(jnp.float32)
    local_first = jnp.dot(member_float, tile_first * factor, precision=lax.Precision.HIGHEST)
    local_second = jnp.dot(
        member_float, tile_second * factor * factor, precision=lax.Precision.HIGHEST
    )
    got_peak, got_first, got_second, got_count = (
        lax.all_to_all(local_peak[:, None, :], "samp", split_axis=0, concat_axis=1, tiled=True),
        lax.all_to_all(local_first[:, None, :], "samp", split_axis=0, concat_axis=1, tiled=True),
        lax.all_to_all(local_second[:, None, :], "samp", split_axis=0, concat_axis=1, tiled=True),
        lax.all_to_all(live_count[:, None, None], "samp", split_axis=0, concat_axis=1, tiled=True),
    )
    event_peak = jnp.max(got_peak, axis=1)
    rescale = jnp.exp(got_peak - event_peak[:, None, :])
    first_sum = jnp.sum(got_first * rescale, axis=1)
    second_sum = jnp.sum(got_second * rescale * rescale, axis=1)
    total_live = jnp.sum(got_count[:, :, 0], axis=1)
    log_evidence = event_peak + jnp.log(first_sum) - jnp.log(total_live)[:, None]
    ess_fraction = first_sum * first_sum / (second_sum * total_live[:, None])
    loglik = lax.psum(jnp.sum(log_evidence, axis=0), "samp") / jnp.float32(EVENTS)
    local_top = jnp.max(loglik)
    grid_top = lax.pmax(local_top, "grid")
    grid_mass = lax.psum(jnp.sum(jnp.exp(loglik - grid_top)), "grid")
    log_posterior = loglik - (grid_top + jnp.log(grid_mass))
    return (log_evidence, ess_fraction, log_posterior)


def solution(mesh):
    in_specs = (P("samp", None), P(None, "grid"), P("grid"), P("samp"), P("samp"), P("samp"))
    out_specs = (P("samp", "grid"), P("samp", "grid"), P("grid"))
    devices = mesh.shape["samp"]

    def body(summary, kernel, *rest):
        tiles, cols = rest[2].shape[0], kernel.shape[1]
        fits = (
            mesh.shape["grid"] == 1
            and cols == devices * LANES
            and cols % (2 * BLOCK) == 0
            and summary.shape[0] == tiles * LANES
            and tiles % 8 == 0
            and EVENTS % devices == 0
        )
        if fits:
            return column_body(devices, summary, kernel, *rest)
        return row_body(summary, kernel, *rest)

    return jax.shard_map(body, mesh=mesh, in_specs=in_specs, out_specs=out_specs, check_vma=False)
```

```python
import functools

import jax
import jax.numpy as jnp
from jax import lax
from jax.experimental import pallas as pl
from jax.experimental.pallas import tpu as pltpu
from jax.sharding import PartitionSpec as P

EVENTS = 64
LANES = 128
GROUP = 16
CHUNK = 128
BLOCK = 1024
UNROLL = 4
NEG = -1e30
DEAD = 1e30
LOG2E = 1.4426950408889634
LN2 = 0.6931471805599453


def stats_kernel(
    tiles, tile_rows, depth, cols, event_hbm, live_hbm, offset_hbm, prior_hbm, summary_ref, kernel_ref,
    out_hbm, built, raw, lhs, rhs, prior, score_a, score_b, top, peak, held_sums, offset_ref, prior_ref,
    event_ref, live_ref, owner, fresh, start, row_sem, col_sem, fact_sem, out_sem,
):
    blocks = cols // BLOCK
    per_tile = tile_rows // GROUP
    sizes = [1 << k for k in reversed(range(per_tile.bit_length()))]
    stride = 2 * tiles + 1
    lanes = BLOCK // LANES
    span = 8 * tiles + 8
    peak_span = tiles + 8
    parts = lanes // 2
    chunk_groups = CHUNK // GROUP

    facts = [
        pltpu.make_async_copy(source, target, fact_sem.at[k])
        for k, (source, target) in enumerate(
            ((live_hbm, live_ref), (event_hbm, event_ref), (prior_hbm, prior_ref), (offset_hbm, offset_ref))
        )
    ]
    for copy in facts:
        copy.start()

    def col_copy(n):
        return pltpu.make_async_copy(kernel_ref.at[:, pl.ds(n * BLOCK, BLOCK)], rhs.at[n], col_sem.at[n])

    col_copy(0).start()

    def row_copies(act):
        for t in range(tiles):
            count = lax.div(live_ref[t] + (GROUP - 1), GROUP)
            base = start[t]
            for k, size in enumerate(sizes):
                done = lax.bitwise_and(count, ~(2 * size - 1))

                @pl.when(lax.bitwise_and(count, size) != 0)
                def _():
                    copy = pltpu.make_async_copy(
                        summary_ref.at[pl.ds(pl.multiple_of(t * tile_rows + done * GROUP, GROUP), size * GROUP)],
                        raw.at[pl.ds(pl.multiple_of((base + done) * GROUP, GROUP), size * GROUP)],
                        row_sem.at[t, k],
                    )
                    act(copy)

    facts[0].wait()
    total = jnp.int32(0)
    for t in range(tiles):
        start[t] = total
        total = total + lax.div(live_ref[t] + (GROUP - 1), GROUP)
    row_copies(lambda copy: copy.start())
    for n in range(1, blocks):
        col_copy(n).start()
    for copy in facts[1:]:
        copy.wait()

    chunks = lax.div(total + (chunk_groups - 1), chunk_groups)
    for t in range(tiles):
        count = lax.div(live_ref[t] + (GROUP - 1), GROUP)

        def mark(j, carry):
            owner[start[t] + j] = t
            fresh[start[t] + j] = jnp.where(j == 0, jnp.float32(0), jnp.float32(1))
            return carry

        lax.fori_loop(0, count, mark, 0)
        row_at = lax.broadcasted_iota(jnp.int32, (1, tile_rows), 1)
        held = jnp.where(row_at < live_ref[t], prior_ref[t : t + 1, :] * jnp.float32(LOG2E), jnp.float32(DEAD))
        spread = jnp.broadcast_to(held, (LANES, tile_rows)).T
        prior[pl.ds(pl.multiple_of(start[t] * GROUP, GROUP), tile_rows), :] = spread
    for j in range(chunk_groups):
        owner[total + j] = tiles
        fresh[total + j] = jnp.float32(0)

    lane_at = lax.broadcasted_iota(jnp.int32, (1, LANES), 1)
    known = jnp.zeros((1, LANES), jnp.float32)
    for t in range(tiles):
        known = jnp.where(lane_at == t, event_ref[t].astype(jnp.float32), known)
        known = jnp.where(lane_at == tiles + t, live_ref[t].astype(jnp.float32), known)
    for d in range(cols // LANES):
        built[d * stride + 2 * tiles : d * stride + 2 * tiles + 1, :] = known

    top[...] = jnp.zeros(top.shape, jnp.float32)
    held_sums[...] = jnp.zeros(held_sums.shape, jnp.float32)
    peak[...] = jnp.zeros(peak.shape, jnp.float32)
    row_copies(lambda copy: copy.wait())

    def rows_at(c, g):
        return pl.ds(pl.multiple_of(c * CHUNK, CHUNK) + g * GROUP, GROUP)

    def tops_open(c):
        base = pl.multiple_of(owner[c * chunk_groups] * 8, 8)
        return [top[pl.ds(base + lane * span, 8), :] for lane in range(lanes)]

    def products(n, c, count, score, h, held):
        at = pl.ds(pl.multiple_of(c * CHUNK, CHUNK), count * CHUNK)
        rows = jnp.concatenate([lhs[k, at, :] for k in range(depth // LANES)], axis=1)
        part = jnp.dot(rows, rhs[n, :, h * 256 : (h + 1) * 256], preferred_element_type=jnp.float32)
        for g in range(count * chunk_groups):
            base = pl.multiple_of(owner[c * chunk_groups + g] * 8, 8)
            reset = fresh[c * chunk_groups + g] * jnp.float32(DEAD) - jnp.float32(DEAD)
            cost = prior[rows_at(c, g), :]
            for w in range(2):
                lane = h * 2 + w
                value = part[g * GROUP : (g + 1) * GROUP, w * LANES : (w + 1) * LANES] * jnp.float32(LOG2E) - cost
                score[rows_at(c, g), lane * LANES : (lane + 1) * LANES] = value
                held[lane] = jnp.maximum(held[lane] + reset, jnp.maximum(value[:8], value[8:]))
                top[pl.ds(base + lane * span, 8), :] = held[lane]

    def sums_open(c):
        base = pl.multiple_of(owner[c * chunk_groups] * 8, 8)
        return [
            [held_sums[pl.ds(base + (k * lanes + lane) * span, 8), :] for lane in range(lanes)] for k in range(2)
        ]

    def sums(c, count, score, part, held):
        one, two = held
        total_groups = count * chunk_groups
        for g in range(part * total_groups // parts, (part + 1) * total_groups // parts):
            tile = owner[c * chunk_groups + g]
            base = pl.multiple_of(tile * 8, 8)
            keep = fresh[c * chunk_groups + g]
            for lane in range(lanes):
                level = peak[pl.ds(tile + lane * peak_span, 8, stride=0), :]
                value = score[rows_at(c, g), lane * LANES : (lane + 1) * LANES]
                low, high = jnp.exp2(value[:8] - level), jnp.exp2(value[8:] - level)
                one[lane] = one[lane] * keep + (low + high)
                two[lane] = two[lane] * keep + (low * low + high * high)
                held_sums[pl.ds(base + lane * span, 8), :] = one[lane]
                held_sums[pl.ds(base + (lanes + lane) * span, 8), :] = two[lane]

    def fold(ref, half, w, join):
        kept = [ref[pl.ds(w * span + half * 64 + i, 8, stride=8), :] for i in range(8)]
        while len(kept) > 1:
            kept = [join(a, b) for a, b in zip(kept[::2], kept[1::2])]
        return kept[0]

    def close_top():
        for half in range(tiles // 8):
            for w in range(lanes):
                peak[pl.ds(w * peak_span + half * 8, 8), :] = fold(top, half, w, jnp.maximum)

    def close_sums(n):
        for half in range(tiles // 8):
            for w in range(lanes):
                one = fold(held_sums, half, w, jnp.add)
                two = fold(held_sums, half, lanes + w, jnp.add)
                level = peak[pl.ds(w * peak_span + half * 8, 8), :]
                shift = offset_ref[:, pl.ds(pl.multiple_of(n * BLOCK + w * LANES, LANES), LANES)]
                base = (n * lanes + w) * stride + half * 8
                built[pl.ds(base, 8), :] = level * jnp.float32(LN2) + jnp.log(one) + shift
                built[pl.ds(base + tiles, 8), :] = two / (one * one)

    def out_copy(n):
        size = lanes * stride
        at = pl.ds(pl.multiple_of(n * size, 8), size)
        return pltpu.make_async_copy(built.at[at], out_hbm.at[at], out_sem.at[n])

    def each_chunk(work):
        def step(i, carry):
            work(i * UNROLL, UNROLL)
            return carry

        lax.fori_loop(0, lax.div(chunks, UNROLL), step, 0)
        count = UNROLL // 2
        while count:
            first = lax.bitwise_and(chunks, ~(2 * count - 1))

            @pl.when(lax.bitwise_and(chunks, count) != 0)
            def _(first=first, count=count):
                work(first, count)

            count //= 2

    def only_products(c, count):
        held = tops_open(c)
        for g in range(count * chunk_groups):
            at = rows_at(c, g)
            for k in range(depth // LANES):
                lhs[k, at, :] = raw[at, k * LANES : (k + 1) * LANES]
        for h in range(parts):
            products(0, c, count, score_a, h, held)

    def only_sums(c, count):
        held = sums_open(c)
        for h in range(parts):
            sums(c, count, score_b, h, held)

    col_copy(0).wait()
    each_chunk(only_products)

    def step(n, now, before):
        close_top()
        col_copy(n).wait()

        def work(c, count):
            held = sums_open(c)
            tops = tops_open(c)
            for h in range(parts):
                sums(c, count, before, h, held)
                products(n, c, count, now, h, tops)

        each_chunk(work)
        close_sums(n - 1)
        out_copy(n - 1).start()

    def pair(i, carry):
        step(2 * i + 1, score_b, score_a)

        @pl.when(i < blocks // 2 - 1)
        def _():
            step(2 * i + 2, score_a, score_b)

        return carry

    lax.fori_loop(0, blocks // 2, pair, 0)
    close_top()
    each_chunk(only_sums)
    close_sums(blocks - 1)
    out_copy(blocks - 1).start()
    for n in range(blocks):
        out_copy(n).wait()


def tile_stats(summary, kernel, grid_offset, log_prior, tile_event, tile_live):
    rows, depth = summary.shape
    cols = kernel.shape[1]
    tiles = tile_event.shape[0]
    tile_rows = rows // tiles
    stride = 2 * tiles + 1
    hbm = pl.BlockSpec(memory_space=pltpu.HBM)
    f32 = jnp.float32
    lanes = BLOCK // LANES
    groups = (rows + CHUNK) // GROUP
    return pl.pallas_call(
        functools.partial(stats_kernel, tiles, tile_rows, depth, cols),
        out_shape=jax.ShapeDtypeStruct((cols // LANES * stride, LANES), f32),
        in_specs=[hbm] * 6,
        out_specs=hbm,
        scratch_shapes=[
            pltpu.VMEM((cols // LANES * stride, LANES), f32),
            pltpu.VMEM((rows + CHUNK, depth), jnp.bfloat16),
            pltpu.VMEM((depth // LANES, rows + CHUNK, LANES), jnp.bfloat16),
            pltpu.VMEM((cols // BLOCK, depth, BLOCK), jnp.bfloat16),
            pltpu.VMEM((rows + CHUNK, LANES), f32),
            pltpu.VMEM((rows + CHUNK, BLOCK), f32),
            pltpu.VMEM((rows + CHUNK, BLOCK), f32),
            pltpu.VMEM((lanes * (8 * tiles + 8), LANES), f32),
            pltpu.VMEM((lanes * (tiles + 8), LANES), f32),
            pltpu.VMEM((2 * lanes * (8 * tiles + 8), LANES), f32),
            pltpu.VMEM((1, cols), f32),
            pltpu.VMEM((tiles, tile_rows), f32),
            pltpu.SMEM((tiles,), jnp.int32),
            pltpu.SMEM((tiles,), jnp.int32),
            pltpu.SMEM((groups,), jnp.int32),
            pltpu.SMEM((groups,), f32),
            pltpu.SMEM((tiles,), jnp.int32),
            pltpu.SemaphoreType.DMA((tiles, (tile_rows // GROUP).bit_length())),
            pltpu.SemaphoreType.DMA((cols // BLOCK,)),
            pltpu.SemaphoreType.DMA((4,)),
            pltpu.SemaphoreType.DMA((cols // BLOCK,)),
        ],
        compiler_params=pltpu.CompilerParams(vmem_limit_bytes=60 << 20),
    )(
        tile_event, tile_live, grid_offset.reshape(1, cols), log_prior.reshape(tiles, tile_rows), summary, kernel,
    )


def split3(x):
    high = x.astype(jnp.bfloat16)
    rest = x - high.astype(jnp.float32)
    middle = rest.astype(jnp.bfloat16)
    low = (rest - middle.astype(jnp.float32)).astype(jnp.bfloat16)
    return high, middle, low


def merge_kernel(devices, tiles, got_ref, out_ref, level, event, peak, kept):
    stride = 2 * tiles + 1
    total = devices * tiles
    facts = got_ref[pl.ds(2 * tiles, devices, stride=stride), :]
    for i in range(tiles):
        at = slice(i * devices, (i + 1) * devices)
        level[at, :] = got_ref[pl.ds(i, devices, stride=stride), :]
        event[at, :] = jnp.broadcast_to(facts[:, i : i + 1], (devices, LANES))
    peak[...] = jnp.zeros(peak.shape, jnp.float32)

    def find(step, carry):
        names = [(step * 4 + k).astype(jnp.float32) for k in range(4)]
        parts = [[jnp.full((8, LANES), NEG, jnp.float32) for _ in range(2)] for _ in range(4)]
        for v in range(total // 8):
            at = slice(v * 8, v * 8 + 8)
            whose, value = event[at, :], level[at, :]
            for k in range(4):
                parts[k][v % 2] = jnp.maximum(
                    parts[k][v % 2], jnp.where(whose == names[k], value, jnp.float32(NEG))
                )
        for k in range(4):
            best = jnp.max(jnp.maximum(parts[k][0], parts[k][1]), axis=0, keepdims=True)
            peak[pl.ds(step * 4 + k, 1), :] = best
        return carry

    lax.fori_loop(0, EVENTS // 4, find, 0)
    names = lax.broadcasted_iota(jnp.int32, (total, LANES), 1).astype(jnp.float32)
    chosen = jnp.where(event[...] == names, jnp.float32(1), jnp.float32(0)).astype(jnp.bfloat16)
    found = jnp.dot(chosen, jnp.concatenate(split3(peak[...]), axis=1), preferred_element_type=jnp.float32)
    shift = (found[:, :LANES] + found[:, LANES : 2 * LANES]) + found[:, 2 * LANES :]
    one = jnp.exp(level[...] - shift)
    ratio = [got_ref[pl.ds(tiles + i, devices, stride=stride), :] for i in range(tiles)]
    two = jnp.concatenate(ratio, axis=0) * one * one
    live = [jnp.broadcast_to(facts[:, tiles + i : tiles + i + 1], (devices, LANES)) for i in range(tiles)]
    live = jnp.concatenate(live, axis=0).astype(jnp.bfloat16)
    right = jnp.concatenate(split3(one) + split3(two) + (live,), axis=1)
    sums = lax.dot_general(chosen, right, (((0,), (0,)), ((), ())), preferred_element_type=jnp.float32)
    part = [sums[:EVENTS, k * LANES : (k + 1) * LANES] for k in range(7)]
    first = part[0] + part[1] + part[2]
    second = part[3] + part[4] + part[5]
    count = part[6]
    evidence = peak[:EVENTS, :] + jnp.log(first) - jnp.log(count)
    kept[:EVENTS, :] = evidence
    kept[EVENTS:, :] = first * first / (second * count)
    own = EVENTS // devices
    out_stride = 2 * own + 1
    for k in range(own):
        out_ref[pl.ds(k, devices, stride=out_stride), :] = kept[pl.ds(k, devices, stride=own), :]
        out_ref[pl.ds(own + k, devices, stride=out_stride), :] = kept[pl.ds(EVENTS + k, devices, stride=own), :]
    loglik = jnp.sum(evidence, axis=0, keepdims=True) / jnp.float32(EVENTS)
    out_ref[pl.ds(2 * own, devices, stride=out_stride), :] = jnp.broadcast_to(loglik, (devices, LANES))


def merge(got, devices, tiles):
    total = devices * tiles
    f32 = jnp.float32
    vmem = pl.BlockSpec(memory_space=pltpu.VMEM)
    return pl.pallas_call(
        functools.partial(merge_kernel, devices, tiles),
        out_shape=jax.ShapeDtypeStruct((devices * (2 * (EVENTS // devices) + 1), LANES), f32),
        in_specs=[vmem],
        out_specs=vmem,
        scratch_shapes=[
            pltpu.VMEM((total, LANES), f32),
            pltpu.VMEM((total, LANES), f32),
            pltpu.VMEM((LANES, LANES), f32),
            pltpu.VMEM((2 * EVENTS, LANES), f32),
        ],
        compiler_params=pltpu.CompilerParams(vmem_limit_bytes=8 << 20),
    )(got)


def last_kernel(devices, own, got_ref, evidence_ref, ess_ref, posterior_ref):
    stride = 2 * own + 1
    for d in range(devices):
        lane = slice(d * LANES, (d + 1) * LANES)
        evidence_ref[:, lane] = got_ref[d * stride : d * stride + own, :]
        ess_ref[:, lane] = got_ref[d * stride + own : d * stride + 2 * own, :]
    loglik = got_ref[pl.ds(2 * own, devices, stride=stride), :]
    top = jnp.max(jnp.max(loglik, axis=0, keepdims=True), axis=1, keepdims=True)
    mass = jnp.exp(loglik - top)
    mass = jnp.sum(jnp.sum(mass, axis=0, keepdims=True), axis=1, keepdims=True)
    posterior_ref[...] = loglik - (top + jnp.log(mass))


def last(got, devices, own):
    f32 = jnp.float32
    vmem = pl.BlockSpec(memory_space=pltpu.VMEM)
    cols = devices * LANES
    return pl.pallas_call(
        functools.partial(last_kernel, devices, own),
        out_shape=(
            jax.ShapeDtypeStruct((own, cols), f32),
            jax.ShapeDtypeStruct((own, cols), f32),
            jax.ShapeDtypeStruct((devices, LANES), f32),
        ),
        in_specs=[vmem],
        out_specs=(vmem, vmem, vmem),
        compiler_params=pltpu.CompilerParams(vmem_limit_bytes=8 << 20),
    )(got)


def exchange(x, devices):
    width = x.shape[0] // devices * LANES
    got = lax.all_to_all(x.reshape(devices, 1, width), "samp", split_axis=0, concat_axis=0, tiled=True)
    return got.reshape(x.shape)


def column_body(devices, summary, kernel, grid_offset, log_prior, tile_event, tile_live):
    tiles = tile_event.shape[0]
    own = EVENTS // devices
    sent = tile_stats(summary, kernel, grid_offset, log_prior, tile_event, tile_live)
    merged = merge(exchange(sent, devices), devices, tiles)
    evidence, ess, posterior = last(exchange(merged, devices), devices, own)
    return evidence, ess, posterior.reshape(-1)


def row_body(summary, kernel, grid_offset, log_prior, tile_event, tile_live):
    row_count = summary.shape[0]
    grid_cols = kernel.shape[1]
    tile_count = tile_event.shape[0]
    tile_rows = row_count // tile_count
    scores = jnp.dot(summary, kernel, preferred_element_type=jnp.float32)
    scores = scores + grid_offset[None, :] - log_prior[:, None]
    scores = scores.reshape(tile_count, tile_rows, grid_cols)
    is_live = lax.broadcasted_iota(jnp.int32, (tile_count, tile_rows), 1) < tile_live[:, None]
    masked = jnp.where(is_live[:, :, None], scores, jnp.float32(-1e30))
    tile_max = jnp.max(masked, axis=1)
    shifted = jnp.exp(masked - tile_max[:, None, :])
    tile_first = jnp.sum(shifted, axis=1)
    tile_second = jnp.sum(shifted * shifted, axis=1)
    member = tile_event[None, :] == lax.broadcasted_iota(jnp.int32, (EVENTS, tile_count), 0)
    local_peak = jnp.max(
        jnp.where(member[:, :, None], tile_max[None, :, :], jnp.float32(-1e30)), axis=1
    )
    live_count = jnp.sum(jnp.where(member, tile_live[None, :], 0), axis=1).astype(jnp.float32)
    factor = jnp.exp(tile_max - local_peak[tile_event])
    member_float = member.astype(jnp.float32)
    local_first = jnp.dot(member_float, tile_first * factor, precision=lax.Precision.HIGHEST)
    local_second = jnp.dot(
        member_float, tile_second * factor * factor, precision=lax.Precision.HIGHEST
    )
    got_peak, got_first, got_second, got_count = (
        lax.all_to_all(local_peak[:, None, :], "samp", split_axis=0, concat_axis=1, tiled=True),
        lax.all_to_all(local_first[:, None, :], "samp", split_axis=0, concat_axis=1, tiled=True),
        lax.all_to_all(local_second[:, None, :], "samp", split_axis=0, concat_axis=1, tiled=True),
        lax.all_to_all(live_count[:, None, None], "samp", split_axis=0, concat_axis=1, tiled=True),
    )
    event_peak = jnp.max(got_peak, axis=1)
    rescale = jnp.exp(got_peak - event_peak[:, None, :])
    first_sum = jnp.sum(got_first * rescale, axis=1)
    second_sum = jnp.sum(got_second * rescale * rescale, axis=1)
    total_live = jnp.sum(got_count[:, :, 0], axis=1)
    log_evidence = event_peak + jnp.log(first_sum) - jnp.log(total_live)[:, None]
    ess_fraction = first_sum * first_sum / (second_sum * total_live[:, None])
    loglik = lax.psum(jnp.sum(log_evidence, axis=0), "samp") / jnp.float32(EVENTS)
    local_top = jnp.max(loglik)
    grid_top = lax.pmax(local_top, "grid")
    grid_mass = lax.psum(jnp.sum(jnp.exp(loglik - grid_top)), "grid")
    log_posterior = loglik - (grid_top + jnp.log(grid_mass))
    return (log_evidence, ess_fraction, log_posterior)


def solution(mesh):
    in_specs = (P("samp", None), P(None, "grid"), P("grid"), P("samp"), P("samp"), P("samp"))
    out_specs = (P("samp", "grid"), P("samp", "grid"), P("grid"))
    devices = mesh.shape["samp"]

    def body(summary, kernel, *rest):
        tiles, cols = rest[2].shape[0], kernel.shape[1]
        fits = (
            mesh.shape["grid"] == 1
            and cols == devices * LANES
            and cols % (2 * BLOCK) == 0
            and summary.shape[0] == tiles * LANES
            and tiles % 8 == 0
            and EVENTS % devices == 0
        )
        if fits:
            return column_body(devices, summary, kernel, *rest)
        return row_body(summary, kernel, *rest)

    return jax.shard_map(body, mesh=mesh, in_specs=in_specs, out_specs=out_specs, check_vma=False)
```
